256 devices in a mesh: dom: 64 (over z_lo, x, y), sub: 4 (over z_hi, core).
Axes of the slice: x: 4, y: 4, z: 8 (z_hi: 2, z_lo: 4; z = z_hi * 4 + z_lo), core: 2. Of those that a mesh axis runs over, the one named last changes fastest.
Arguments:
- positions: bfloat16 [3, 32768], P(None, ('dom', 'sub')), may hold values from 0 to 1
- species: int32 [32768], P(('dom', 'sub')), may hold values from 0 to 1
- neighbours: int32 [64, 32768], P(None, ('dom', 'sub')), may hold values from -1 to 255, as said below
- ghost_rows: int32 [4, 8192], P(None, ('dom', 'sub')), may hold values from 0 to 127
- wavevectors: int32 [3, 12288], replicated, may hold values from -19 to 20, as said below
- embedding: bfloat16 [2, 128], replicated, may hold values from -6 to 6
- w_in: bfloat16 [2, 128, 128], replicated, may hold values from -0.5 to 0.5
- radial: bfloat16 [2, 8, 128], replicated, may hold values from -2 to 2
- norm_gain: bfloat16 [2, 128], replicated, may hold values from 0.25 to 1.75
- w_out: bfloat16 [2, 128, 128], replicated, may hold values from -0.5 to 0.5
- w_charge: bfloat16 [128, 8], replicated, may hold values from -0.5 to 0.5
Outputs:
- potentials: float32 [8, 32768], P(None, ('dom', 'sub'))
- forces: float32 [3, 32768], P(None, ('dom', 'sub'))
The draws below stay inside these ranges and needn't reach their ends.
Inputs may be any that keep to these rules, and one draw needn't show every extreme that they name: `neighbours`: used slots come first in each atom's list, -1 fills the rest, and every list uses 64 // 2 slots or more; an entry below 128 is one of the device's own atoms, else it is ghost number (entry - 128) % 32 of block (entry - 128) // 32 of the table. `wavevectors`: the columns are distinct; the first nonzero component of each column is positive; the sum of the squares of a column is at most 400.
All inputs are finite; a program needn't handle non-finite values.
Results may differ from the reference program's by a relative error of at most 0.0067.
Values may be sent and summed in bfloat16 or wider, within the bound.
A program may use at most 64 MiB of HBM per device.

```python
import math
import jax
import jax.numpy as jnp
from jax import lax

C = 128
B = 8
Q = 8
K = 12288
NB = 64
LAYERS = 2
REACH = 20
A = 128
G = 32
ATOMS = 32768
N_DOM = 64
N_SUB = 4
DEVICES = 256


def draw_neighbours(key, part):
    key_kind, key_local, key_ghost, key_count = jax.random.split(jax.random.fold_in(key, 11), 4)
    kind = jax.random.randint(key_kind, (NB, ATOMS), 0, 8)
    local = jax.random.randint(key_local, (NB, ATOMS), 0, A)
    ghost = jax.random.randint(key_ghost, (NB, ATOMS), 0, G)
    count = jax.random.randint(key_count, (1, ATOMS), NB // 2, NB + 1)
    entry = jnp.where(kind < 4, local, A + (kind - 4) * G + ghost)
    slot_number = jnp.arange(NB, dtype=jnp.int32)[:, None]
    return jnp.where(slot_number < count, entry, -1).astype(jnp.int32)


def draw_wavevectors(key, part):
    side_len = 2 * REACH + 1
    shuffled = jax.random.permutation(jax.random.fold_in(key, 23), side_len * side_len * side_len).astype(jnp.int32)
    first_comp = shuffled // (side_len * side_len) - REACH
    second_comp = shuffled // side_len % side_len - REACH
    third_comp = shuffled % side_len - REACH
    squared = first_comp * first_comp + second_comp * second_comp + third_comp * third_comp
    upper_half = (first_comp > 0) | (first_comp == 0) & (second_comp > 0) | (first_comp == 0) & (second_comp == 0) & (third_comp > 0)
    inside = upper_half & (squared <= REACH * REACH)
    top_end = (first_comp == REACH) & (second_comp == 0) & (third_comp == 0)
    low_end = (first_comp == 1) & (second_comp == 1 - REACH) & (third_comp == 0)
    order_key = jnp.where(top_end | low_end, 0, jnp.where(inside, 1, 2)).astype(jnp.int32)
    chosen_rows = jnp.argsort(order_key, stable=True)[:K]
    return jnp.stack([first_comp[chosen_rows], second_comp[chosen_rows], third_comp[chosen_rows]]).astype(jnp.int32)


def touch_ends(values, stream_key, smallest, top_value):
    place = [jax.random.randint(jax.random.fold_in(stream_key, axis), (), 0, length) for axis, length in enumerate(values.shape)]
    longest = values.shape.index(max(values.shape))
    next_to = place[:longest] + [(place[longest] + 1) % values.shape[longest]] + place[longest + 1:]
    return values.at[tuple(place)].set(smallest).at[tuple(next_to)].set(top_value)


def steps_of(key, extent, shards, low, largest):
    loudness, own = 1.0, jax.random.fold_in(key, 6)
    for position, blocks in shards:
        draws = jnp.exp(jax.random.uniform(jax.random.fold_in(own, position), (blocks,), jnp.float32, low / len(shards), largest / len(shards)))
        loudness = loudness * jnp.repeat(draws, extent[position] // blocks).reshape([-1 if axis == position else 1 for axis in range(len(extent))])
    return loudness


def centred(key, shape, scale, most, held_as=jnp.bfloat16):
    return jnp.clip(scale * jax.random.normal(key, shape, jnp.float32), -most, most).astype(held_as)


def setup_inputs(seed: int = 0) -> dict:
    keys = jax.random.split(jax.random.key(seed), 12)
    positions = jnp.clip(1.0 * jax.random.uniform(keys[0], (3, ATOMS), jnp.float32) ** steps_of(keys[0], (3, ATOMS), ((1, 256),), -0.2, 0.2), 0.0, 1.0).astype(jnp.bfloat16)
    species = touch_ends(jax.random.randint(keys[1], (ATOMS,), 0, 2), jax.random.fold_in(keys[1], 1), 0, 1).astype(jnp.int32)
    neighbours = draw_neighbours(jax.random.fold_in(keys[11], 71), 0)
    ghost_rows = touch_ends(jax.random.randint(keys[3], (4, G * DEVICES), 0, A), jax.random.fold_in(keys[3], 1), 0, A - 1).astype(jnp.int32)
    wavevectors = draw_wavevectors(jax.random.fold_in(keys[11], 71), 0)
    embedding = centred(keys[5], (2, C), 1.0, 6.0)
    w_in = centred(keys[6], (LAYERS, C, C), C ** -0.5, 0.5)
    radial = centred(keys[7], (LAYERS, B, C), B ** -0.5, 2.0)
    norm_gain = jnp.clip(1.0 + 0.15 * jax.random.normal(keys[8], (LAYERS, C), jnp.float32), 0.25, 1.75).astype(jnp.bfloat16)
    w_out = centred(keys[9], (LAYERS, C, C), C ** -0.5, 0.5)
    w_charge = centred(keys[10], (C, Q), C ** -0.5, 0.5)
    return dict(positions=positions, species=species, neighbours=neighbours, ghost_rows=ghost_rows, wavevectors=wavevectors, embedding=embedding, w_in=w_in, radial=radial, norm_gain=norm_gain, w_out=w_out, w_charge=w_charge)


smearing = 0.005
epsilon = 1e-05
highest = lax.Precision.HIGHEST

def reference(positions, species, neighbours, ghost_rows, wavevectors, embedding, w_in, radial, norm_gain, w_out, w_charge):
    devices = N_DOM * N_SUB
    table_rows = A + 4 * G
    ghost_grid = ghost_rows.reshape(4, N_DOM, N_SUB, G)

    def with_ghosts(local):
        width = local.shape[3]
        picked = []
        for side_number in range(4):
            index_grid = jnp.broadcast_to(ghost_grid[side_number][:, :, :, None], (N_DOM, N_SUB, G, width))
            picked.append(jnp.take_along_axis(local, index_grid, axis=2))
        joined = jnp.concatenate([local, jnp.roll(picked[1], 1, axis=0), jnp.roll(picked[0], -1, axis=0), jnp.roll(picked[3], 1, axis=1), jnp.roll(picked[2], -1, axis=1)], axis=2)
        return joined.reshape(devices, table_rows, width)
    local_coords = positions.reshape(3, N_DOM, N_SUB, A).transpose(1, 2, 3, 0)
    coord_table = with_ghosts(local_coords).astype(jnp.float32)
    lists = neighbours.reshape(NB, devices, A).transpose(1, 0, 2)
    clamped = jnp.maximum(lists, 0)
    live_mask = lists >= 0
    own_coords = positions.astype(jnp.float32).reshape(3, devices, A).transpose(1, 2, 0)
    nearby = jax.vmap(lambda table, chosen: table[chosen])(coord_table, clamped)
    displace = nearby - own_coords[:, None, :, :]
    chord_sq = lax.optimization_barrier(jnp.sum(jnp.sin(math.pi * displace) ** 2, axis=3))
    decay_rates = jnp.exp2(jnp.arange(B, dtype=jnp.float32) - 3.0)
    radial_basis = jnp.exp(-decay_rates[None, :, None, None] * chord_sq[:, None, :, :])
    hidden = jnp.where((species == 1)[:, None], embedding[1][None, :], embedding[0][None, :])
    for layer_number in range(LAYERS):
        projected = jnp.dot(hidden.astype(jnp.float32), w_in[layer_number].astype(jnp.float32), precision=highest, preferred_element_type=jnp.float32).astype(jnp.bfloat16)
        feat_tables = with_ghosts(projected.reshape(N_DOM, N_SUB, A, C))
        radial_layer = radial[layer_number].astype(jnp.float32)

        def one_device(inputs):
            basis_here, clamped_here, live_here, table_here = inputs
            edge_weight = jnp.einsum('bna,bc->nac', basis_here, radial_layer, precision=highest)
            gathered = table_here[clamped_here].astype(jnp.float32)
            return lax.optimization_barrier(jnp.sum(jnp.where(live_here[:, :, None], edge_weight * gathered, 0.0), axis=0))
        message = lax.map(one_device, (radial_basis, clamped, live_mask, feat_tables)).reshape(ATOMS, C)
        normed = message * lax.rsqrt(lax.optimization_barrier(jnp.mean(message * message, axis=1, keepdims=True)) + epsilon)
        normed = normed * norm_gain[layer_number].astype(jnp.float32)[None, :]
        activated = jax.nn.silu(normed).astype(jnp.bfloat16)
        update = jnp.dot(activated.astype(jnp.float32), w_out[layer_number].astype(jnp.float32), precision=highest, preferred_element_type=jnp.float32)
        hidden = (hidden.astype(jnp.float32) + update).astype(jnp.bfloat16)
    charges = jnp.dot(hidden.astype(jnp.float32), w_charge.astype(jnp.float32), precision=highest, preferred_element_type=jnp.float32).T
    wave_float = wavevectors.astype(jnp.float32)
    squared = lax.optimization_barrier(jnp.sum(wave_float * wave_float, axis=0))
    kweight = jnp.exp(-smearing * squared) / squared
    coords = positions.astype(jnp.float32)
    block_len = math.gcd(K, 128)
    block_count = K // block_len
    wave_blocks = wave_float.reshape(3, block_count, block_len).transpose(1, 0, 2)

    def phases(chosen):
        angle = 2.0 * math.pi * jnp.einsum('dk,da->ka', chosen, coords, precision=highest)
        return (jnp.cos(angle), jnp.sin(angle))

    def structure_block(chosen):
        cosines, sines = phases(chosen)
        return jnp.concatenate([jnp.einsum('qa,ka->qk', charges, cosines, precision=highest), jnp.einsum('qa,ka->qk', charges, sines, precision=highest)], axis=0)
    structure = lax.map(structure_block, wave_blocks)
    weighted = structure * kweight.reshape(block_count, 1, block_len)

    def apply_block(carry, inputs):
        potential, force_sum = carry
        chosen, weight_block = inputs
        cosines, sines = phases(chosen)
        cos_weight = weight_block[:Q]
        sin_weight = weight_block[Q:]
        potential = potential + jnp.einsum('qk,ka->qa', cos_weight, cosines, precision=highest)
        potential = potential + jnp.einsum('qk,ka->qa', sin_weight, sines, precision=highest)
        cos_dir = chosen[:, None, :] * cos_weight[None, :, :]
        sin_dir = chosen[:, None, :] * sin_weight[None, :, :]
        inner = jnp.einsum('dqk,ka->dqa', cos_dir, sines, precision=highest)
        inner = inner - jnp.einsum('dqk,ka->dqa', sin_dir, cosines, precision=highest)
        force_sum = force_sum + lax.optimization_barrier(jnp.sum(charges[None, :, :] * inner, axis=1))
        return ((potential, force_sum), None)
    start = (jnp.zeros((Q, ATOMS), jnp.float32), jnp.zeros((3, ATOMS), jnp.float32))
    (potential, force_sum), _ = lax.scan(apply_block, start, (wave_blocks, weighted))
    scale = 1.0 / math.sqrt(ATOMS)
    return (potential * scale, force_sum * scale)
```

```python
import functools
import math

import jax
import jax.numpy as jnp
import numpy as np
from jax import lax
from jax.experimental import pallas as pl
from jax.experimental.pallas import tpu as pltpu
from jax.sharding import PartitionSpec as P

MESH = pl.DeviceIdType.MESH
smearing = 0.005
epsilon = 1e-05
f32 = jnp.float32
bf16 = jnp.bfloat16
plane = 16
members = 2 * plane
depth = 8
round_magic = 12582912.0


def fit_series(function, terms):
    nodes = (np.cos(np.pi * (np.arange(4 * terms) + 0.5) / (4 * terms)) + 1.0) / 8.0
    fitted = np.polynomial.chebyshev.Chebyshev.fit(nodes, function(np.sqrt(nodes)), terms - 1, domain=[0.0, 0.25])
    return [float(c) for c in fitted.convert(kind=np.polynomial.Polynomial).coef]


def cos_series(terms):
    return fit_series(lambda t: np.cos(2.0 * np.pi * t), terms)


def sin_series(terms):
    return fit_series(lambda t: np.sin(2.0 * np.pi * t) / t, terms)


def horner(coefs, u):
    value = coefs[-1]
    for c in coefs[-2::-1]:
        value = value * u + c
    return value


def turns_cos_sin(turns, cos_coefs, sin_coefs):
    t = turns - ((turns + round_magic) - round_magic)
    u = t * t
    return horner(cos_coefs, u), t * horner(sin_coefs, u)


def dot_nt(a, b):
    return lax.dot_general(a, b, (((1,), (1,)), ((), ())), preferred_element_type=f32)


def dot_nn(a, b):
    return jnp.dot(a, b, preferred_element_type=f32)


def kernel(
    scale,
    pos_ref, spec_ref, nbr_ref, gr_ref, wv_ref, emb_ref, win_ref, rad_ref, gain_ref, wout_ref, wch_ref,
    pot_ref, force_ref,
    c32, coords, ghost_out, ghost_in, gpad, pos_all, q_all, wv32, wvb, wvt,
    cos_s, sin_s, cos_a, sin_a, m_ref, feat_out, feat_in, z_out, z_in, z_full,
    g1_send, g1_recv, g2_send, g2_recv, p_send, p_recv, q_send, q_recv,
    zs_send, zs_recv, w_send, w_recv, x_send, x_recv,
):
    dom = lax.axis_index("dom")
    sub = lax.axis_index("sub")
    n_dom = lax.axis_size("dom")
    n_sub = lax.axis_size("sub")
    zl, xy = dom // plane, lax.rem(dom, plane)
    zh, core = sub // 2, lax.rem(sub, 2)
    me = core * plane + xy
    z_me = zh * (depth // 2) + zl
    atoms = pos_ref.shape[1]
    total_k = wv_ref.shape[1]
    share = total_k // members
    latent = wch_ref.shape[1]
    bases = rad_ref.shape[1]
    ghosts = gr_ref.shape[1]

    def member(index):
        return (zl * plane + lax.rem(index, plane), zh * 2 + index // plane)

    def column_member(index):
        return (lax.rem(index, depth // 2) * plane + xy, (index // (depth // 2)) * 2 + core)

    neighbours_at = (
        (lax.rem(dom + 1, n_dom), sub),
        (lax.rem(dom + n_dom - 1, n_dom), sub),
        (dom, lax.rem(sub + 1, n_sub)),
        (dom, lax.rem(sub + n_sub - 1, n_sub)),
    )

    barrier = pltpu.get_barrier_semaphore()
    for target in neighbours_at:
        pl.semaphore_signal(barrier, inc=1, device_id=target, device_id_type=MESH)

    @pl.loop(1, members)
    def _(o):
        pl.semaphore_signal(barrier, inc=1, device_id=member(lax.rem(me + o, members)), device_id_type=MESH)

    @pl.loop(1, depth)
    def _(o):
        pl.semaphore_signal(barrier, inc=1, device_id=column_member(lax.rem(z_me + o, depth)), device_id_type=MESH)

    c32[...] = jnp.zeros_like(c32)
    c32[0:3, :] = pos_ref[...].astype(f32)
    c32[3:4, :] = spec_ref[...].astype(f32)
    coords[...] = c32[...].astype(bf16)
    gpad[...] = jnp.zeros_like(gpad)
    gpad[0:4, 0:ghosts] = gr_ref[...].astype(f32)
    grown = gpad[...]
    picks = grown[1:2, :]
    for block, source in ((1, 0), (2, 3), (3, 2)):
        picks = picks + pltpu.roll(grown, block * ghosts, axis=1)[source:source + 1, :]
    row_number = lax.broadcasted_iota(jnp.int32, (atoms, atoms), 0).astype(f32)
    pick_cols = jnp.where(row_number == picks, 1.0, 0.0)
    ghost_out[...] = dot_nn(coords[...], pick_cols.astype(bf16)).astype(bf16)
    my_lanes = pl.ds(pl.multiple_of(me * atoms, atoms), atoms)
    pos_all[:, my_lanes] = coords[...]

    def ghost_copy(block):
        return pltpu.make_async_remote_copy(
            src_ref=ghost_out, dst_ref=ghost_in.at[block], send_sem=g1_send.at[block], recv_sem=g1_recv.at[block],
            device_id=neighbours_at[block], device_id_type=MESH)

    def feat_copy(block):
        rows = pl.ds(block * ghosts, ghosts)
        return pltpu.make_async_remote_copy(
            src_ref=feat_out.at[rows], dst_ref=feat_in.at[rows], send_sem=g2_send.at[block], recv_sem=g2_recv.at[block],
            device_id=neighbours_at[block], device_id_type=MESH)

    def spread_copy(o, buffer, send, recv, slot):
        lanes = pl.ds(pl.multiple_of(slot * atoms, atoms), atoms)
        return pltpu.make_async_remote_copy(
            src_ref=buffer.at[:, lanes], dst_ref=buffer.at[:, lanes], send_sem=send.at[o], recv_sem=recv.at[o],
            device_id=member(lax.rem(me + o, members)), device_id_type=MESH)

    def spread_start(buffer, send, recv):
        @pl.loop(1, members)
        def _(o):
            spread_copy(o, buffer, send, recv, me).start()

    def spread_wait(buffer, send, recv):
        @pl.loop(1, members)
        def _(o):
            spread_copy(o, buffer, send, recv, lax.rem(me + members - o, members)).wait_recv()

    def spread_sent(buffer, send, recv):
        @pl.loop(1, members)
        def _(o):
            spread_copy(o, buffer, send, recv, me).wait_send()

    def column_copy(o):
        return pltpu.make_async_remote_copy(
            src_ref=z_out, dst_ref=z_in.at[o], send_sem=zs_send.at[o], recv_sem=zs_recv.at[o],
            device_id=column_member(lax.rem(z_me + o, depth)), device_id_type=MESH)

    def share_lanes(which_core, which_xy):
        first = (which_core * plane + which_xy) * share
        return pl.ds(pl.multiple_of(first, 128), share)

    def plane_copy(o, from_xy):
        lanes = share_lanes(core, from_xy)
        return pltpu.make_async_remote_copy(
            src_ref=z_full.at[:, lanes], dst_ref=z_full.at[:, lanes], send_sem=w_send.at[o], recv_sem=w_recv.at[o],
            device_id=(zl * plane + lax.rem(xy + o, plane), sub), device_id_type=MESH)

    def twin_copy(o, from_core):
        lanes = share_lanes(from_core, lax.rem(xy + plane - o, plane))
        return pltpu.make_async_remote_copy(
            src_ref=z_full.at[:, lanes], dst_ref=z_full.at[:, lanes], send_sem=x_send.at[o], recv_sem=x_recv.at[o],
            device_id=(dom, zh * 2 + 1 - core), device_id_type=MESH)

    pl.semaphore_wait(barrier, 4 + (members - 1) + (depth - 1))
    for block in range(4):
        ghost_copy(block).start()
    spread_start(pos_all, p_send, p_recv)

    table_row = lax.broadcasted_iota(jnp.int32, (2 * atoms, atoms), 0)

    def tally(step, counted):
        for inner in range(8):
            counted = counted + jnp.where(table_row == nbr_ref[pl.ds(step * 8 + inner, 1), :], 1.0, 0.0)
        return counted

    counted = lax.fori_loop(0, nbr_ref.shape[0] // 8, tally, jnp.zeros((2 * atoms, atoms), f32))
    counts = (counted[:atoms].T, counted[atoms:].T)
    pick_rows = pick_cols.T.astype(bf16)

    wv32[...] = jnp.zeros_like(wv32)
    wv32[0:3, :] = wv_ref[...].astype(f32)
    wvb[...] = wv32[...].astype(bf16)
    own_share = pl.ds(pl.multiple_of(me * share, 128), share)
    own_waves = wv32[:, own_share]
    wvt[...] = own_waves.T.astype(bf16)
    squared = jnp.sum(own_waves * own_waves, axis=0, keepdims=True)
    kweight = jnp.exp(-smearing * squared) / squared * scale

    cos_fine, sin_fine = cos_series(9), sin_series(9)
    cos_fast, sin_fast = cos_series(6), sin_series(5)

    own32 = c32[...]
    own_cos, own_sin = turns_cos_sin(0.5 * own32, cos_fine, sin_fine)
    own_cos_col, own_sin_col = own_cos.T, own_sin.T
    own_col = own32.T
    pos_col = own_col.astype(bf16)
    embedding = emb_ref[...].astype(f32)
    gains = gain_ref[...].astype(f32)
    is_second = own_col[:, 3:4] > 0.5
    hidden = jnp.where(is_second, embedding[1:2, :], embedding[0:1, :])
    both = lax.broadcasted_iota(jnp.int32, (16, embedding.shape[1]), 0)
    both = jnp.where(both == 1, embedding[1:2, :], embedding[0:1, :]).astype(bf16)
    projected_kinds = dot_nn(both, win_ref[0]).astype(bf16).astype(f32)
    own_feats = jnp.where(is_second, projected_kinds[1:2, :], projected_kinds[0:1, :])
    charge_rows = wch_ref[...].astype(f32).T.astype(bf16)

    def fill_pairs(half, table_cos, table_sin):
        chord = jnp.zeros((atoms, atoms), f32)
        for d in range(3):
            apart = table_sin[d:d + 1, :] * own_cos_col[:, d:d + 1] - table_cos[d:d + 1, :] * own_sin_col[:, d:d + 1]
            chord = chord + apart * apart
        for b in range(bases):
            pair = counts[half] * jnp.exp(-(2.0 ** (b - 3)) * chord)
            high = pair.astype(bf16)
            rows = slice(b * atoms, (b + 1) * atoms)
            m_ref[rows, half * atoms:(half + 1) * atoms] = high
            m_ref[rows, (half + 2) * atoms:(half + 3) * atoms] = (pair - high.astype(f32)).astype(bf16)

    def layer(number, hidden, table):
        products = dot_nn(m_ref[...], jnp.concatenate([table, table], axis=0))
        radial_layer = rad_ref[number].astype(f32)
        message = radial_layer[0:1, :] * products[:atoms]
        for b in range(1, bases):
            message = message + radial_layer[b:b + 1, :] * products[b * atoms:(b + 1) * atoms]
        normed = message * lax.rsqrt(jnp.mean(message * message, axis=1, keepdims=True) + epsilon)
        normed = normed * gains[number:number + 1, :]
        activated = (normed / (1.0 + jnp.exp(-normed))).astype(bf16)
        update = dot_nn(activated, wout_ref[number])
        return (hidden + update).astype(bf16).astype(f32)

    fill_pairs(0, own_cos, own_sin)

    for block in range(4):
        ghost_copy(block).wait_recv()
    lane_block = lax.broadcasted_iota(jnp.int32, (16, atoms), 1) // ghosts
    ghost32 = jnp.zeros((16, atoms), f32)
    for block in range(4):
        ghost32 = jnp.where(lane_block == block, ghost_in[block].astype(f32), ghost32)
    ghost_cos, ghost_sin = turns_cos_sin(0.5 * ghost32, cos_fine, sin_fine)
    fill_pairs(1, ghost_cos, ghost_sin)
    ghost_second = ghost32.T[:, 3:4] > 0.5
    ghost_feats = jnp.where(ghost_second, projected_kinds[1:2, :], projected_kinds[0:1, :])
    table = jnp.concatenate([own_feats, ghost_feats], axis=0).astype(bf16)
    hidden = layer(0, hidden, table)
    projected = dot_nn(hidden.astype(bf16), win_ref[1]).astype(bf16)
    feat_out[...] = dot_nn(pick_rows, projected).astype(bf16)
    for block in range(4):
        feat_copy(block).start()

    spread_wait(pos_all, p_send, p_recv)

    def share_phases(step):
        lanes = pl.ds(pl.multiple_of(step * 256, 256), 256)
        for first in range(0, share, 64):
            rows = slice(first, first + 64)
            cosines, sines = turns_cos_sin(dot_nn(wvt[rows, :], pos_all[:, lanes]), cos_fast, sin_fast)
            cos_s[rows, lanes] = cosines.astype(bf16)
            sin_s[rows, lanes] = sines.astype(bf16)

    def atom_phases(step):
        lanes = pl.ds(pl.multiple_of(step * 256, 256), 256)
        for first in range(0, atoms, 64):
            rows = slice(first, first + 64)
            cosines, sines = turns_cos_sin(dot_nn(pos_col[rows, :], wvb[:, lanes]), cos_fast, sin_fast)
            cos_a[rows, lanes] = cosines.astype(bf16)
            sin_a[rows, lanes] = sines.astype(bf16)

    share_steps = members * atoms // 256
    atom_steps = total_k // 256
    pl.loop(0, share_steps // 2)(share_phases)

    for block in range(4):
        feat_copy(block).wait_recv()
    table = jnp.concatenate([projected, feat_in[...]], axis=0)
    hidden = layer(1, hidden, table)
    charges = dot_nt(charge_rows, hidden.astype(bf16))
    charges_high = charges.astype(bf16).astype(f32)
    q_all[:, my_lanes] = jnp.concatenate([charges_high, charges - charges_high], axis=0).astype(bf16)
    spread_start(q_all, q_send, q_recv)
    pl.loop(share_steps // 2, share_steps)(share_phases)
    spread_wait(q_all, q_send, q_recv)

    by_cos = dot_nt(q_all[...], cos_s[...])
    by_sin = dot_nt(q_all[...], sin_s[...])
    partial = jnp.concatenate([by_cos[:latent] + by_cos[latent:], by_sin[:latent] + by_sin[latent:]], axis=0) * kweight
    z_out[...] = partial.astype(bf16)

    @pl.loop(1, depth)
    def _(o):
        column_copy(o).start()

    pl.loop(0, atom_steps // 2)(atom_phases)

    @pl.loop(1, depth)
    def _(o):
        column_copy(o).wait_recv()

    summed = z_out[...].astype(f32)
    for o in range(1, depth):
        summed = summed + z_in[o].astype(f32)
    z_full[:, share_lanes(core, xy)] = summed.astype(bf16)

    @pl.loop(1, plane)
    def _(o):
        plane_copy(o, xy).start()

    twin_copy(0, core).start()
    pl.loop(atom_steps // 2, atom_steps)(atom_phases)

    @pl.loop(1, plane)
    def _(o):
        plane_copy(o, lax.rem(xy + plane - o, plane)).wait_recv()
        twin_copy(o, core).start()

    @pl.loop(0, plane)
    def _(o):
        twin_copy(o, 1 - core).wait_recv()

    def apply_block(step, sums):
        lanes = pl.ds(pl.multiple_of(step * 512, 512), 512)
        block = z_full[:, lanes].astype(f32)
        waves = wv32[0:8, lanes]
        left = jnp.concatenate([block] + [block * waves[d:d + 1, :] for d in range(3)], axis=0).astype(bf16)
        return sums[0] + dot_nt(left, cos_a[:, lanes]), sums[1] + dot_nt(left, sin_a[:, lanes])

    blank = jnp.zeros((64, atoms), f32)
    by_cos, by_sin = lax.fori_loop(0, total_k // 512, apply_block, (blank, blank))
    pot_ref[...] = by_cos[:latent] + by_sin[latent:2 * latent]
    for d in range(3):
        first = 2 * latent * (d + 1)
        inner = by_sin[first:first + latent] - by_cos[first + latent:first + 2 * latent]
        force_ref[d:d + 1, :] = jnp.sum(charges * inner, axis=0, keepdims=True)

    for block in range(4):
        ghost_copy(block).wait_send()
        feat_copy(block).wait_send()
    spread_sent(pos_all, p_send, p_recv)
    spread_sent(q_all, q_send, q_recv)

    @pl.loop(1, depth)
    def _(o):
        column_copy(o).wait_send()

    @pl.loop(1, plane)
    def _(o):
        plane_copy(o, xy).wait_send()

    @pl.loop(0, plane)
    def _(o):
        twin_copy(o, core).wait_send()


def per_device(positions, species, neighbours, ghost_rows, wavevectors, embedding, w_in, radial, norm_gain, w_out, w_charge):
    atoms = positions.shape[1]
    total_k = wavevectors.shape[1]
    latent = w_charge.shape[1]
    channels = w_in.shape[2]
    bases = radial.shape[1]
    share = total_k // members
    scale = 1.0 / math.sqrt(atoms * lax.axis_size(("dom", "sub")))
    dma = pltpu.SemaphoreType.DMA
    vmem = pl.BlockSpec(memory_space=pltpu.VMEM)
    return pl.pallas_call(
        functools.partial(kernel, scale),
        out_shape=(
            jax.ShapeDtypeStruct((latent, atoms), f32),
            jax.ShapeDtypeStruct((3, atoms), f32),
        ),
        in_specs=[vmem] * 11,
        out_specs=(vmem, vmem),
        scratch_shapes=[
            pltpu.VMEM((16, atoms), f32),
            pltpu.VMEM((16, atoms), bf16),
            pltpu.VMEM((16, atoms), bf16),
            pltpu.VMEM((4, 16, atoms), bf16),
            pltpu.VMEM((8, atoms), f32),
            pltpu.VMEM((16, members * atoms), bf16),
            pltpu.VMEM((16, members * atoms), bf16),
            pltpu.VMEM((16, total_k), f32),
            pltpu.VMEM((16, total_k), bf16),
            pltpu.VMEM((share, 16), bf16),
            pltpu.VMEM((share, members * atoms), bf16),
            pltpu.VMEM((share, members * atoms), bf16),
            pltpu.VMEM((atoms, total_k), bf16),
            pltpu.VMEM((atoms, total_k), bf16),
            pltpu.VMEM((bases * atoms, 4 * atoms), bf16),
            pltpu.VMEM((atoms, channels), bf16),
            pltpu.VMEM((atoms, channels), bf16),
            pltpu.VMEM((16, share), bf16),
            pltpu.VMEM((depth, 16, share), bf16),
            pltpu.VMEM((16, total_k), bf16),
            dma((4,)), dma((4,)), dma((4,)), dma((4,)),
            dma((members,)), dma((members,)), dma((members,)), dma((members,)),
            dma((depth,)), dma((depth,)), dma((plane,)), dma((plane,)), dma((plane,)), dma((plane,)),
        ],
        compiler_params=pltpu.CompilerParams(
            collective_id=0, has_side_effects=True, vmem_limit_bytes=48 * 1024 * 1024
        ),
        name="ewald_step",
    )(
        positions, species.reshape(1, atoms), neighbours, ghost_rows, wavevectors,
        embedding, w_in, radial, norm_gain, w_out, w_charge,
    )


def solution(mesh):
    return jax.shard_map(
        per_device,
        mesh=mesh,
        in_specs=(
            P(None, ("dom", "sub")),
            P(("dom", "sub")),
            P(None, ("dom", "sub")),
            P(None, ("dom", "sub")),
            P(),
            P(),
            P(),
            P(),
            P(),
            P(),
            P(),
        ),
        out_specs=(P(None, ("dom", "sub")), P(None, ("dom", "sub"))),
        check_vma=False,
    )
```

```python
import functools
import math

import jax
import jax.numpy as jnp
import numpy as np
from jax import lax
from jax.experimental import pallas as pl
from jax.experimental.pallas import tpu as pltpu
from jax.sharding import PartitionSpec as P

MESH = pl.DeviceIdType.MESH
smearing = 0.005
epsilon = 1e-05
f32 = jnp.float32
bf16 = jnp.bfloat16
side = 4
plane = side * side
members = 2 * plane
depth = 8
round_magic = 12582912.0


def fit_series(function, terms):
    nodes = (np.cos(np.pi * (np.arange(4 * terms) + 0.5) / (4 * terms)) + 1.0) / 8.0
    fitted = np.polynomial.chebyshev.Chebyshev.fit(nodes, function(np.sqrt(nodes)), terms - 1, domain=[0.0, 0.25])
    return [float(c) for c in fitted.convert(kind=np.polynomial.Polynomial).coef]


def cos_series(terms):
    return fit_series(lambda t: np.cos(2.0 * np.pi * t), terms)


def sin_series(terms):
    return fit_series(lambda t: np.sin(2.0 * np.pi * t) / t, terms)


def horner(coefs, u):
    value = coefs[-1]
    for c in coefs[-2::-1]:
        value = value * u + c
    return value


def turns_cos_sin(turns, cos_coefs, sin_coefs):
    t = turns - ((turns + round_magic) - round_magic)
    u = t * t
    return horner(cos_coefs, u), t * horner(sin_coefs, u)


def dot_nt(a, b):
    return lax.dot_general(a, b, (((1,), (1,)), ((), ())), preferred_element_type=f32)


def dot_nn(a, b):
    return jnp.dot(a, b, preferred_element_type=f32)


def torus_offsets():
    every = [(dx, dy, dc) for dx in range(side) for dy in range(side) for dc in range(2)]
    return sorted(every, key=lambda o: (min(o[0], side - o[0]) + min(o[1], side - o[1]), o))


def opposite(offset):
    return (-offset[0] % side, -offset[1] % side, offset[2])


def kernel(
    scale,
    pos_hbm, spec_hbm, gr_hbm, nbr_hbm, wv_hbm, emb_hbm, win_hbm, rad_hbm, gain_hbm, wout_hbm, wch_hbm,
    out_ref,
    pos_ref, spec_ref, gr_ref, nbr_ref, wv_ref, emb_ref, win_ref, rad_ref, gain_ref, wout_ref, wch_ref,
    c32, coords, ghost_out, ghost_in, gpad, pos_all, q_all, wv32, share_waves,
    share_phase, atom_phase, pairs_own, pairs_ghost, feat_out, feat_in, z_out, z_in, z_full, left,
    in_sem, g1_send, g1_recv, g2_send, g2_recv, p_send, p_recv, q_send, q_recv,
    zs_send, zs_recv, w_send, w_recv, x_send, x_recv,
):
    dom = lax.axis_index("dom")
    sub = lax.axis_index("sub")
    n_dom = lax.axis_size("dom")
    n_sub = lax.axis_size("sub")
    zl, xy = dom // plane, lax.rem(dom, plane)
    my_x, my_y = xy // side, lax.rem(xy, side)
    zh, core = sub // 2, lax.rem(sub, 2)
    z_me = zh * (depth // 2) + zl
    atoms = pos_ref.shape[1]
    total_k = wv_ref.shape[1]
    share = total_k // members
    half_k = total_k // 2
    latent = wch_ref.shape[0]
    bases = rad_ref.shape[1]
    ghosts = gr_ref.shape[1]

    def member(offset):
        dx, dy, dc = offset
        chip = lax.rem(my_x + dx, side) * side + lax.rem(my_y + dy, side)
        return (zl * plane + chip, zh * 2 + (1 - core if dc else core))

    def column_member(dz):
        index = lax.rem(z_me + dz, depth)
        return (lax.rem(index, depth // 2) * plane + xy, (index // (depth // 2)) * 2 + core)

    neighbours_at = (
        (lax.rem(dom + 1, n_dom), sub),
        (lax.rem(dom + n_dom - 1, n_dom), sub),
        (dom, lax.rem(sub + 1, n_sub)),
        (dom, lax.rem(sub + n_sub - 1, n_sub)),
    )
    offsets = torus_offsets()
    slot_of = {offset: slot for slot, offset in enumerate(offsets)}
    chip_offsets = [offset for offset in offsets if offset[2] == 0]
    heights = sorted(range(1, depth), key=lambda dz: -min(dz, depth - dz))

    fetches = [
        pltpu.make_async_copy(source, target, in_sem.at[number])
        for number, (source, target) in enumerate((
            (pos_hbm, pos_ref), (spec_hbm, spec_ref), (gr_hbm, gr_ref), (nbr_hbm, nbr_ref), (wv_hbm, wv_ref),
            (emb_hbm, emb_ref), (win_hbm, win_ref), (rad_hbm, rad_ref), (gain_hbm, gain_ref), (wout_hbm, wout_ref),
            (wch_hbm, wch_ref)))
    ]
    barrier = pltpu.get_barrier_semaphore()

    def greet(target):
        pl.semaphore_signal(barrier, inc=1, device_id=target, device_id_type=MESH)

    for target in neighbours_at[::-1]:
        greet(target)
    for fetch in fetches[:3]:
        fetch.start()
    for offset in offsets[:0:-1]:
        greet(member(offset))
    for dz in heights:
        greet(column_member(dz))
    for fetch in fetches[3:]:
        fetch.start()

    c32[...] = jnp.zeros_like(c32)
    gpad[...] = jnp.zeros_like(gpad)
    for fetch in fetches[:3]:
        fetch.wait()
    c32[0:3, :] = pos_ref[...].astype(f32)
    c32[3:4, :] = spec_ref[...].astype(f32)
    own32 = c32[...]
    coords[...] = own32.astype(bf16)
    gpad[0:4, 0:ghosts] = gr_ref[...].astype(f32)
    grown = gpad[...]
    picks = grown[1:2, :]
    for block, source in ((1, 0), (2, 3), (3, 2)):
        picks = picks + pltpu.roll(grown, block * ghosts, axis=1)[source:source + 1, :]
    row_number = lax.broadcasted_iota(jnp.int32, (atoms, atoms), 0).astype(f32)
    pick_cols = jnp.where(row_number == picks, 1.0, 0.0)
    ghost_out[...] = dot_nn(own32.astype(bf16), pick_cols.astype(bf16)).astype(bf16)
    pos_all[:, 0:atoms] = own32.astype(bf16)

    def ghost_copy(block):
        return pltpu.make_async_remote_copy(
            src_ref=ghost_out, dst_ref=ghost_in.at[block], send_sem=g1_send, recv_sem=g1_recv,
            device_id=neighbours_at[block], device_id_type=MESH)

    def feat_copy(block):
        rows = pl.ds(block * ghosts, ghosts)
        return pltpu.make_async_remote_copy(
            src_ref=feat_out.at[rows], dst_ref=feat_in.at[rows], send_sem=g2_send, recv_sem=g2_recv,
            device_id=neighbours_at[block], device_id_type=MESH)

    def slot_lanes(first, count):
        return pl.ds(first * atoms, count * atoms)

    near_count = members // 2

    def spread_copy(buffer, send, recv, offset):
        landing = slot_of[opposite(offset)]
        return pltpu.make_async_remote_copy(
            src_ref=buffer.at[:, slot_lanes(0, 1)], dst_ref=buffer.at[:, slot_lanes(landing, 1)],
            send_sem=send, recv_sem=recv.at[0 if landing < near_count else 1],
            device_id=member(offset), device_id_type=MESH)

    def spread_all(buffer, send, recv, first, count, group):
        lanes = slot_lanes(first, count)
        return pltpu.make_async_remote_copy(
            src_ref=buffer.at[:, lanes], dst_ref=buffer.at[:, lanes], send_sem=send, recv_sem=recv.at[group],
            device_id=member(offsets[1]), device_id_type=MESH)

    def spread_start(buffer, send, recv):
        for offset in offsets[:0:-1]:
            spread_copy(buffer, send, recv, offset).start()

    def spread_near(buffer, send, recv):
        spread_all(buffer, send, recv, 1, near_count - 1, 0).wait_recv()

    def spread_far(buffer, send, recv):
        spread_all(buffer, send, recv, near_count, members - near_count, 1).wait_recv()

    def spread_sent(buffer, send, recv):
        spread_all(buffer, send, recv, 1, members - 1, 0).wait_send()

    def column_copy(dz):
        return pltpu.make_async_remote_copy(
            src_ref=z_out, dst_ref=z_in.at[dz - 1], send_sem=zs_send, recv_sem=zs_recv,
            device_id=column_member(dz), device_id_type=MESH)

    column_all = pltpu.make_async_remote_copy(
        src_ref=z_in, dst_ref=z_in, send_sem=zs_send, recv_sem=zs_recv,
        device_id=column_member(1), device_id_type=MESH)

    def chip_share(offset, which_core):
        chip = lax.rem(my_x + offset[0], side) * side + lax.rem(my_y + offset[1], side)
        return pl.ds(pl.multiple_of((which_core * plane + chip) * share, 128), share)

    def plane_copy(number, owner):
        lanes = chip_share(owner, core)
        return pltpu.make_async_remote_copy(
            src_ref=z_full.at[:, lanes], dst_ref=z_full.at[:, lanes], send_sem=w_send, recv_sem=w_recv.at[number],
            device_id=member(chip_offsets[number]), device_id_type=MESH)

    plane_all = pltpu.make_async_remote_copy(
        src_ref=z_full.at[:, pl.ds(0, (plane - 1) * share)], dst_ref=z_full.at[:, pl.ds(0, (plane - 1) * share)],
        send_sem=w_send, recv_sem=w_recv.at[0], device_id=member(chip_offsets[1]), device_id_type=MESH)
    twin = (dom, zh * 2 + 1 - core)

    def twin_copy(offset):
        lanes = chip_share(offset, core)
        return pltpu.make_async_remote_copy(
            src_ref=z_full.at[:, lanes], dst_ref=z_full.at[:, lanes], send_sem=x_send, recv_sem=x_recv,
            device_id=twin, device_id_type=MESH)

    twin_all = pltpu.make_async_remote_copy(
        src_ref=z_full.at[:, pl.ds(0, half_k)], dst_ref=z_full.at[:, pl.ds(0, half_k)],
        send_sem=x_send, recv_sem=x_recv, device_id=twin, device_id_type=MESH)
    ghost_all = pltpu.make_async_remote_copy(
        src_ref=ghost_in, dst_ref=ghost_in, send_sem=g1_send, recv_sem=g1_recv, device_id=twin, device_id_type=MESH)
    feat_all = pltpu.make_async_remote_copy(
        src_ref=feat_in, dst_ref=feat_in, send_sem=g2_send, recv_sem=g2_recv, device_id=twin, device_id_type=MESH)

    pl.semaphore_wait(barrier, 4 + (members - 1) + (depth - 1))
    for block in (3, 2, 1, 0):
        ghost_copy(block).start()
    spread_start(pos_all, p_send, p_recv)

    for fetch in fetches[3:]:
        fetch.wait()
    listed = nbr_ref[...]
    quarters = []
    for first in range(0, 2 * atoms, 64):
        table_row = lax.broadcasted_iota(jnp.int32, (64, atoms), 0) + first
        counted = jnp.zeros((64, atoms), f32)
        for slot in range(listed.shape[0]):
            counted = jnp.where(table_row == listed[slot:slot + 1, :], counted + 1.0, counted)
        quarters.append(counted)
    own_counts = jnp.concatenate(quarters[:2], axis=0).T
    ghost_counts = jnp.concatenate(quarters[2:], axis=0).T
    pick_rows = pick_cols.T.astype(bf16)

    cos_fine, sin_fine = cos_series(9), sin_series(9)
    cos_fast, sin_fast = cos_series(6), sin_series(5)
    own_cos, own_sin = turns_cos_sin(0.5 * own32, cos_fine, sin_fine)
    own_cos_col, own_sin_col = own_cos.T, own_sin.T
    embedding = emb_ref[...].astype(f32)
    gains = gain_ref[...].astype(f32)
    is_second = own32.T[:, 3:4] > 0.5
    hidden = jnp.where(is_second, embedding[1:2, :], embedding[0:1, :])
    both = lax.broadcasted_iota(jnp.int32, (16, embedding.shape[1]), 0)
    both = jnp.where(both == 1, embedding[1:2, :], embedding[0:1, :]).astype(bf16)
    projected_kinds = dot_nn(both, win_ref[0]).astype(bf16).astype(f32)
    own_feats = jnp.where(is_second, projected_kinds[1:2, :], projected_kinds[0:1, :]).astype(bf16)

    def fill_pairs(pairs, counts, table_cos, table_sin):
        chord = jnp.zeros((atoms, atoms), f32)
        for d in range(3):
            apart = table_sin[d:d + 1, :] * own_cos_col[:, d:d + 1] - table_cos[d:d + 1, :] * own_sin_col[:, d:d + 1]
            chord = chord + apart * apart
        basis = jnp.exp(-0.125 * chord)
        for b in range(bases):
            pair = counts * basis
            high = pair.astype(bf16)
            rows = slice(b * atoms, (b + 1) * atoms)
            pairs[rows, 0:atoms] = high
            pairs[rows, atoms:2 * atoms] = (pair - high.astype(f32)).astype(bf16)
            basis = basis * basis

    def messages(number, pairs, feats):
        products = dot_nn(pairs[...], jnp.concatenate([feats, feats], axis=0))
        radial_layer = rad_ref[number].astype(f32)
        message = radial_layer[0:1, :] * products[:atoms]
        for b in range(1, bases):
            message = message + radial_layer[b:b + 1, :] * products[b * atoms:(b + 1) * atoms]
        return message

    def update(number, hidden, message):
        normed = message * lax.rsqrt(jnp.mean(message * message, axis=1, keepdims=True) + epsilon)
        normed = normed * gains[number:number + 1, :]
        activated = (normed / (1.0 + jnp.exp(-normed))).astype(bf16)
        return (hidden + dot_nn(activated, wout_ref[number])).astype(bf16)

    fill_pairs(pairs_own, own_counts, own_cos, own_sin)
    own_message = messages(0, pairs_own, own_feats)

    wv32[...] = jnp.zeros_like(wv32)
    wv32[0:3, :] = wv_ref[...].astype(f32)
    own_waves = wv32[:, chip_share((0, 0), core)]
    share_waves[0:8, :] = own_waves
    share_waves[8:16, :] = jnp.zeros_like(own_waves)
    squared = jnp.sum(own_waves * own_waves, axis=0, keepdims=True)
    kweight = jnp.exp(-smearing * squared) / squared * scale

    ghost_all.wait_recv()
    lane_block = lax.broadcasted_iota(jnp.int32, (16, atoms), 1) // ghosts
    ghost32 = jnp.zeros((16, atoms), f32)
    for block in range(4):
        ghost32 = jnp.where(lane_block == block, ghost_in[block].astype(f32), ghost32)
    ghost_cos, ghost_sin = turns_cos_sin(0.5 * ghost32, cos_fine, sin_fine)
    fill_pairs(pairs_ghost, ghost_counts, ghost_cos, ghost_sin)
    ghost_second = ghost32.T[:, 3:4] > 0.5
    ghost_feats = jnp.where(ghost_second, projected_kinds[1:2, :], projected_kinds[0:1, :]).astype(bf16)
    hidden = update(0, hidden, own_message + messages(0, pairs_ghost, ghost_feats))
    projected = dot_nn(hidden, win_ref[1]).astype(bf16)
    feat_out[...] = dot_nn(pick_rows, projected).astype(bf16)
    for block in (3, 2, 1, 0):
        feat_copy(block).start()
    own_message = messages(1, pairs_own, projected)

    spread_near(pos_all, p_send, p_recv)
    spread_far(pos_all, p_send, p_recv)
    waves16 = share_waves[...].astype(bf16)

    def share_phases(step):
        for part in range(4):
            rows = pl.ds(pl.multiple_of(step * 512 + part * 128, 128), 128)
            places = pos_all[:, rows].astype(f32).T.astype(bf16)
            cosines, sines = turns_cos_sin(dot_nn(places, waves16), cos_fast, sin_fast)
            share_phase[rows, 0:share] = cosines.astype(bf16)
            share_phase[rows, share:2 * share] = sines.astype(bf16)

    def atom_phases(step):
        for part in range(8):
            rows = pl.ds(pl.multiple_of(step * 2048 + part * 256, 256), 256)
            waves = wv32[:, rows].T
            waves = jnp.concatenate([waves, jnp.zeros_like(waves)], axis=1).astype(bf16)
            cosines, sines = turns_cos_sin(dot_nn(waves, coords[...]), cos_fast, sin_fast)
            atom_phase[rows, 0:atoms] = cosines.astype(bf16)
            atom_phase[rows, atoms:2 * atoms] = sines.astype(bf16)

    share_steps = members * atoms // 512
    atom_steps = total_k // 2048
    pl.loop(0, share_steps)(share_phases)
    ghost_all.wait_send()
    spread_sent(pos_all, p_send, p_recv)

    feat_all.wait_recv()
    hidden = update(1, hidden, own_message + messages(1, pairs_ghost, feat_in[...]))
    charges = dot_nt(wch_ref[...], hidden)
    charges_high = charges.astype(bf16).astype(f32)
    q_all[:, 0:atoms] = jnp.concatenate([charges_high, charges - charges_high], axis=0).astype(bf16)
    spread_start(q_all, q_send, q_recv)
    pl.loop(0, atom_steps // 2)(atom_phases)
    feat_all.wait_send()

    near_lanes, far_lanes = slice(0, near_count * atoms), slice(near_count * atoms, members * atoms)
    spread_near(q_all, q_send, q_recv)
    both_parts = dot_nn(q_all[:, near_lanes], share_phase[near_lanes, :])
    spread_far(q_all, q_send, q_recv)
    both_parts = both_parts + dot_nn(q_all[:, far_lanes], share_phase[far_lanes, :])
    both_parts = both_parts[:latent] + both_parts[latent:]
    z_out[...] = (jnp.concatenate([both_parts[:, :share], both_parts[:, share:]], axis=0) * kweight).astype(bf16)
    for dz in heights:
        column_copy(dz).start()
    pl.loop(atom_steps // 2, atom_steps)(atom_phases)
    spread_sent(q_all, q_send, q_recv)

    column_all.wait_recv()
    summed = z_out[...].astype(f32)
    for dz in range(1, depth):
        summed = summed + z_in[dz - 1].astype(f32)
    z_full[:, chip_share((0, 0), core)] = summed.astype(bf16)
    for number in range(plane - 1, 0, -1):
        plane_copy(number, (0, 0)).start()
    twin_copy((0, 0)).start()
    column_all.wait_send()
    for number in range(1, plane):
        source = opposite(chip_offsets[number])
        plane_copy(number, source).wait_recv()
        twin_copy(source).start()
    plane_all.wait_send()

    def apply_half(which_core):
        start = pl.multiple_of(which_core * half_k, half_k)
        for first in range(0, half_k, 512):
            lanes = pl.ds(pl.multiple_of(start + first, 512), 512)
            block = z_full[:, lanes].astype(f32)
            waves = wv32[:, lanes]
            here = slice(first, first + 512)
            left[0:16, here] = z_full[:, lanes]
            for d in range(3):
                left[16 * (d + 1):16 * (d + 2), here] = (block * waves[d:d + 1, :]).astype(bf16)
        return dot_nn(left[...], atom_phase[pl.ds(start, half_k), :])

    sums = apply_half(core)
    twin_all.wait_recv()
    sums = sums + apply_half(1 - core)
    by_cos, by_sin = sums[:, :atoms], sums[:, atoms:]
    out_ref[...] = jnp.zeros_like(out_ref)
    out_ref[0:latent, :] = by_cos[:latent] + by_sin[latent:2 * latent]
    for d in range(3):
        first = 2 * latent * (d + 1)
        inner = by_sin[first:first + latent] - by_cos[first + latent:first + 2 * latent]
        out_ref[latent + d:latent + d + 1, :] = jnp.sum(charges * inner, axis=0, keepdims=True)
    twin_all.wait_send()


def per_device(positions, species, neighbours, ghost_rows, wavevectors, embedding, w_in, radial, norm_gain, w_out, w_charge):
    atoms = positions.shape[1]
    total_k = wavevectors.shape[1]
    latent = w_charge.shape[1]
    channels = w_in.shape[2]
    bases = radial.shape[1]
    share = total_k // members
    scale = 1.0 / math.sqrt(atoms * lax.axis_size(("dom", "sub")))
    operands = (
        positions, species.reshape(1, atoms), ghost_rows, neighbours, wavevectors,
        embedding, w_in, radial, norm_gain, w_out, w_charge.T,
    )
    dma = pltpu.SemaphoreType.DMA
    vmem = pl.BlockSpec(memory_space=pltpu.VMEM)
    hbm = pl.BlockSpec(memory_space=pltpu.HBM)
    packed = pl.pallas_call(
        functools.partial(kernel, scale),
        out_shape=jax.ShapeDtypeStruct((16, atoms), f32),
        in_specs=[hbm] * len(operands),
        out_specs=vmem,
        scratch_shapes=[pltpu.VMEM(value.shape, value.dtype) for value in operands] + [
            pltpu.VMEM((16, atoms), f32),
            pltpu.VMEM((16, atoms), bf16),
            pltpu.VMEM((16, atoms), bf16),
            pltpu.VMEM((4, 16, atoms), bf16),
            pltpu.VMEM((8, atoms), f32),
            pltpu.VMEM((16, members * atoms), bf16),
            pltpu.VMEM((16, members * atoms), bf16),
            pltpu.VMEM((8, total_k), f32),
            pltpu.VMEM((16, share), f32),
            pltpu.VMEM((members * atoms, 2 * share), bf16),
            pltpu.VMEM((total_k, 2 * atoms), bf16),
            pltpu.VMEM((bases * atoms, 2 * atoms), bf16),
            pltpu.VMEM((bases * atoms, 2 * atoms), bf16),
            pltpu.VMEM((atoms, channels), bf16),
            pltpu.VMEM((atoms, channels), bf16),
            pltpu.VMEM((16, share), bf16),
            pltpu.VMEM((depth - 1, 16, share), bf16),
            pltpu.VMEM((16, total_k), bf16),
            pltpu.VMEM((64, total_k // 2), bf16),
            dma((len(operands),)), dma, dma, dma, dma, dma, dma((2,)), dma, dma((2,)),
            dma, dma, dma, dma((plane,)), dma, dma,
        ],
        compiler_params=pltpu.CompilerParams(
            collective_id=0, has_side_effects=True, vmem_limit_bytes=60 * 1024 * 1024
        ),
        name="ewald_step",
    )(*operands)
    return packed[:latent], packed[latent:latent + 3]


def solution(mesh):
    return jax.shard_map(
        per_device,
        mesh=mesh,
        in_specs=(
            P(None, ("dom", "sub")),
            P(("dom", "sub")),
            P(None, ("dom", "sub")),
            P(None, ("dom", "sub")),
            P(),
            P(),
            P(),
            P(),
            P(),
            P(),
            P(),
        ),
        out_specs=(P(None, ("dom", "sub")), P(None, ("dom", "sub"))),
        check_vma=False,
    )
```

```python
import functools
import math

import jax
import jax.numpy as jnp
import numpy as np
from jax import lax
from jax.experimental import pallas as pl
from jax.experimental.pallas import tpu as pltpu
from jax.sharding import PartitionSpec as P

MESH = pl.DeviceIdType.MESH
smearing = 0.005
epsilon = 1e-05
f32 = jnp.float32
bf16 = jnp.bfloat16
side = 4
plane = side * side
members = 2 * plane
depth = 8
round_magic = 12582912.0


def fit_series(function, terms):
    nodes = (np.cos(np.pi * (np.arange(4 * terms) + 0.5) / (4 * terms)) + 1.0) / 8.0
    fitted = np.polynomial.chebyshev.Chebyshev.fit(nodes, function(np.sqrt(nodes)), terms - 1, domain=[0.0, 0.25])
    return [float(c) for c in fitted.convert(kind=np.polynomial.Polynomial).coef]


def cos_series(terms):
    return fit_series(lambda t: np.cos(2.0 * np.pi * t), terms)


def sin_series(terms):
    return fit_series(lambda t: np.sin(2.0 * np.pi * t) / t, terms)


def horner(coefs, u):
    value = coefs[-1]
    for c in coefs[-2::-1]:
        value = value * u + c
    return value


def turns_cos_sin(turns, cos_coefs, sin_coefs):
    t = turns - ((turns + round_magic) - round_magic)
    u = t * t
    return horner(cos_coefs, u), t * horner(sin_coefs, u)


def dot_nt(a, b):
    return lax.dot_general(a, b, (((1,), (1,)), ((), ())), preferred_element_type=f32)


def dot_nn(a, b):
    return jnp.dot(a, b, preferred_element_type=f32)


def torus_offsets():
    every = [(dx, dy, dc) for dx in range(side) for dy in range(side) for dc in range(2)]
    return sorted(every, key=lambda o: (min(o[0], side - o[0]) + min(o[1], side - o[1]), o))


def opposite(offset):
    return (-offset[0] % side, -offset[1] % side, offset[2])


def kernel(
    scale,
    pos_hbm, spec_hbm, gr_hbm, nbr_hbm, wv_hbm, emb_hbm, win_hbm, rad_hbm, gain_hbm, wout_hbm, wch_hbm,
    out_ref,
    pos_ref, spec_ref, gr_ref, nbr_ref, wv_ref, emb_ref, win_ref, rad_ref, gain_ref, wout_ref, wch_ref,
    c32, ghost_out, ghost_in, gpad, pos_all, q_all, wv32,
    share_phase, atom_phase, pairs_own, pairs_ghost, feat_out, feat_in, z_out, z_in, z_full, left,
    in_sem, g1_send, g1_recv, g2_send, g2_recv, p_send, p_recv, q_send, q_recv,
    zs_send, zs_recv, w_send, w_recv, x_send, x_recv,
):
    dom = lax.axis_index("dom")
    sub = lax.axis_index("sub")
    n_dom = lax.axis_size("dom")
    n_sub = lax.axis_size("sub")
    zl, xy = dom // plane, lax.rem(dom, plane)
    my_x, my_y = xy // side, lax.rem(xy, side)
    zh, core = sub // 2, lax.rem(sub, 2)
    z_me = zh * (depth // 2) + zl
    atoms = pos_ref.shape[1]
    total_k = wv_ref.shape[1]
    share = total_k // members
    latent = wch_ref.shape[0]
    bases = rad_ref.shape[1]
    ghosts = gr_ref.shape[1]

    def member(offset):
        dx, dy, dc = offset
        chip = lax.rem(my_x + dx, side) * side + lax.rem(my_y + dy, side)
        return (zl * plane + chip, zh * 2 + (1 - core if dc else core))

    def column_member(dz):
        index = lax.rem(z_me + dz, depth)
        return (lax.rem(index, depth // 2) * plane + xy, (index // (depth // 2)) * 2 + core)

    neighbours_at = (
        (lax.rem(dom + 1, n_dom), sub),
        (lax.rem(dom + n_dom - 1, n_dom), sub),
        (dom, lax.rem(sub + 1, n_sub)),
        (dom, lax.rem(sub + n_sub - 1, n_sub)),
    )
    offsets = torus_offsets()
    slot_of = {offset: slot for slot, offset in enumerate(offsets)}
    chip_offsets = [offset for offset in offsets if offset[2] == 0]
    heights = sorted(range(1, depth), key=lambda dz: -min(dz, depth - dz))

    fetches = [
        pltpu.make_async_copy(source, target, in_sem.at[number])
        for number, (source, target) in enumerate((
            (pos_hbm, pos_ref), (spec_hbm, spec_ref), (gr_hbm, gr_ref), (nbr_hbm, nbr_ref), (wv_hbm, wv_ref),
            (emb_hbm, emb_ref), (win_hbm, win_ref), (rad_hbm, rad_ref), (gain_hbm, gain_ref), (wout_hbm, wout_ref),
            (wch_hbm, wch_ref)))
    ]
    barrier = pltpu.get_barrier_semaphore()

    def greet(target):
        pl.semaphore_signal(barrier, inc=1, device_id=target, device_id_type=MESH)

    for target in neighbours_at[::-1]:
        greet(target)
    for fetch in fetches[:3]:
        fetch.start()
    for offset in offsets[:0:-1]:
        greet(member(offset))
    for dz in heights:
        greet(column_member(dz))
    for fetch in fetches[3:]:
        fetch.start()

    c32[...] = jnp.zeros_like(c32)
    gpad[...] = jnp.zeros_like(gpad)
    for fetch in fetches[:3]:
        fetch.wait()
    c32[0:3, :] = pos_ref[...].astype(f32)
    c32[3:4, :] = spec_ref[...].astype(f32)
    own32 = c32[...]
    own_coords = own32.astype(bf16)
    gpad[0:4, 0:ghosts] = gr_ref[...].astype(f32)
    grown = gpad[...]
    picks = grown[1:2, :]
    for block, source in ((1, 0), (2, 3), (3, 2)):
        picks = picks + pltpu.roll(grown, block * ghosts, axis=1)[source:source + 1, :]
    row_number = lax.broadcasted_iota(jnp.int32, (atoms, atoms), 0).astype(f32)
    pick_cols = jnp.where(row_number == picks, 1.0, 0.0)
    ghost_out[...] = dot_nn(own_coords, pick_cols.astype(bf16)).astype(bf16)
    pos_all[:, 0:atoms] = own_coords

    def ghost_copy(block):
        return pltpu.make_async_remote_copy(
            src_ref=ghost_out, dst_ref=ghost_in.at[block], send_sem=g1_send, recv_sem=g1_recv,
            device_id=neighbours_at[block], device_id_type=MESH)

    def feat_copy(block):
        rows = pl.ds(block * ghosts, ghosts)
        return pltpu.make_async_remote_copy(
            src_ref=feat_out.at[rows], dst_ref=feat_in.at[rows], send_sem=g2_send, recv_sem=g2_recv,
            device_id=neighbours_at[block], device_id_type=MESH)

    def slot_lanes(first, count):
        return pl.ds(first * atoms, count * atoms)

    near_count = members // 2

    def spread_copy(buffer, send, recv, offset):
        landing = slot_of[opposite(offset)]
        return pltpu.make_async_remote_copy(
            src_ref=buffer.at[:, slot_lanes(0, 1)], dst_ref=buffer.at[:, slot_lanes(landing, 1)],
            send_sem=send, recv_sem=recv.at[0 if landing < near_count else 1],
            device_id=member(offset), device_id_type=MESH)

    def spread_all(buffer, send, recv, first, count, group):
        lanes = slot_lanes(first, count)
        return pltpu.make_async_remote_copy(
            src_ref=buffer.at[:, lanes], dst_ref=buffer.at[:, lanes], send_sem=send, recv_sem=recv.at[group],
            device_id=member(offsets[1]), device_id_type=MESH)

    def spread_start(buffer, send, recv):
        for offset in offsets[:0:-1]:
            spread_copy(buffer, send, recv, offset).start()

    def spread_near(buffer, send, recv):
        spread_all(buffer, send, recv, 1, near_count - 1, 0).wait_recv()

    def spread_far(buffer, send, recv):
        spread_all(buffer, send, recv, near_count, members - near_count, 1).wait_recv()

    def spread_sent(buffer, send, recv):
        spread_all(buffer, send, recv, 1, members - 1, 0).wait_send()

    def column_copy(dz):
        return pltpu.make_async_remote_copy(
            src_ref=z_out, dst_ref=z_in.at[dz - 1], send_sem=zs_send, recv_sem=zs_recv,
            device_id=column_member(dz), device_id_type=MESH)

    column_all = pltpu.make_async_remote_copy(
        src_ref=z_in, dst_ref=z_in, send_sem=zs_send, recv_sem=zs_recv,
        device_id=column_member(1), device_id_type=MESH)

    def share_lanes(first, count):
        return pl.ds(first * share, count * share)

    def plane_copy(number):
        landing = chip_offsets.index(opposite(chip_offsets[number]))
        return pltpu.make_async_remote_copy(
            src_ref=z_full.at[:, share_lanes(0, 1)], dst_ref=z_full.at[:, share_lanes(landing, 1)],
            send_sem=w_send, recv_sem=w_recv.at[landing], device_id=member(chip_offsets[number]), device_id_type=MESH)

    def plane_arrival(slot):
        lanes = share_lanes(slot, 1)
        return pltpu.make_async_remote_copy(
            src_ref=z_full.at[:, lanes], dst_ref=z_full.at[:, lanes], send_sem=w_send, recv_sem=w_recv.at[slot],
            device_id=member(chip_offsets[1]), device_id_type=MESH)

    plane_all = pltpu.make_async_remote_copy(
        src_ref=z_full.at[:, share_lanes(1, plane - 1)], dst_ref=z_full.at[:, share_lanes(1, plane - 1)],
        send_sem=w_send, recv_sem=w_recv.at[0], device_id=member(chip_offsets[1]), device_id_type=MESH)
    twin = (dom, zh * 2 + 1 - core)
    rings = ((0, 5), (5, 11), (11, plane))

    def twin_copy(slot):
        ring = [first <= slot < last for first, last in rings].index(True)
        return pltpu.make_async_remote_copy(
            src_ref=z_full.at[:, share_lanes(slot, 1)], dst_ref=z_full.at[:, share_lanes(plane + slot, 1)],
            send_sem=x_send, recv_sem=x_recv.at[ring], device_id=twin, device_id_type=MESH)

    def twin_arrival(ring):
        first, last = rings[ring]
        lanes = share_lanes(plane + first, last - first)
        return pltpu.make_async_remote_copy(
            src_ref=z_full.at[:, lanes], dst_ref=z_full.at[:, lanes], send_sem=x_send, recv_sem=x_recv.at[ring],
            device_id=twin, device_id_type=MESH)

    twin_all = pltpu.make_async_remote_copy(
        src_ref=z_full.at[:, share_lanes(0, plane)], dst_ref=z_full.at[:, share_lanes(0, plane)],
        send_sem=x_send, recv_sem=x_recv.at[0], device_id=twin, device_id_type=MESH)
    ghost_all = pltpu.make_async_remote_copy(
        src_ref=ghost_in, dst_ref=ghost_in, send_sem=g1_send, recv_sem=g1_recv, device_id=twin, device_id_type=MESH)
    feat_all = pltpu.make_async_remote_copy(
        src_ref=feat_in, dst_ref=feat_in, send_sem=g2_send, recv_sem=g2_recv, device_id=twin, device_id_type=MESH)

    pl.semaphore_wait(barrier, 4 + (members - 1) + (depth - 1))
    for block in (3, 2, 1, 0):
        ghost_copy(block).start()

    for fetch in fetches[3:]:
        fetch.wait()
    listed = nbr_ref[...]
    quarters = []
    for first in range(0, 2 * atoms, 64):
        table_row = lax.broadcasted_iota(jnp.int32, (64, atoms), 0) + first
        counted = jnp.zeros((64, atoms), f32)
        for slot in range(listed.shape[0]):
            counted = jnp.where(table_row == listed[slot:slot + 1, :], counted + 1.0, counted)
        quarters.append(counted)
    own_counts = jnp.concatenate(quarters[:2], axis=0).T
    ghost_counts = jnp.concatenate(quarters[2:], axis=0).T
    pick_rows = pick_cols.T.astype(bf16)

    cos_fine, sin_fine = cos_series(9), sin_series(9)
    cos_fast, sin_fast = cos_series(6), sin_series(5)
    own_cos, own_sin = turns_cos_sin(0.5 * own32, cos_fine, sin_fine)
    own_cos_col, own_sin_col = own_cos.T, own_sin.T
    embedding = emb_ref[...].astype(f32)
    gains = gain_ref[...].astype(f32)
    is_second = own32.T[:, 3:4] > 0.5
    hidden = jnp.where(is_second, embedding[1:2, :], embedding[0:1, :])
    both = lax.broadcasted_iota(jnp.int32, (16, embedding.shape[1]), 0)
    both = jnp.where(both == 1, embedding[1:2, :], embedding[0:1, :]).astype(bf16)
    projected_kinds = dot_nn(both, win_ref[0]).astype(bf16).astype(f32)
    own_feats = jnp.where(is_second, projected_kinds[1:2, :], projected_kinds[0:1, :]).astype(bf16)

    def fill_pairs(pairs, counts, table_cos, table_sin):
        chord = jnp.zeros((atoms, atoms), f32)
        for d in range(3):
            apart = table_sin[d:d + 1, :] * own_cos_col[:, d:d + 1] - table_cos[d:d + 1, :] * own_sin_col[:, d:d + 1]
            chord = chord + apart * apart
        basis = jnp.exp(-0.125 * chord)
        for b in range(bases):
            pair = counts * basis
            high = pair.astype(bf16)
            rows = slice(b * atoms, (b + 1) * atoms)
            pairs[rows, 0:atoms] = high
            pairs[rows, atoms:2 * atoms] = (pair - high.astype(f32)).astype(bf16)
            basis = basis * basis

    def messages(number, pairs, feats):
        products = dot_nn(pairs[...], jnp.concatenate([feats, feats], axis=0))
        radial_layer = rad_ref[number].astype(f32)
        message = radial_layer[0:1, :] * products[:atoms]
        for b in range(1, bases):
            message = message + radial_layer[b:b + 1, :] * products[b * atoms:(b + 1) * atoms]
        return message

    def update(number, hidden, message):
        normed = message * lax.rsqrt(jnp.mean(message * message, axis=1, keepdims=True) + epsilon)
        normed = normed * gains[number:number + 1, :]
        activated = (normed / (1.0 + jnp.exp(-normed))).astype(bf16)
        return (hidden + dot_nn(activated, wout_ref[number])).astype(bf16)

    fill_pairs(pairs_own, own_counts, own_cos, own_sin)
    own_message = messages(0, pairs_own, own_feats)

    wv32[...] = jnp.zeros_like(wv32)
    for slot in range(members):
        dx, dy, _ = chip_offsets[slot % plane]
        chip = lax.rem(my_x + dx, side) * side + lax.rem(my_y + dy, side)
        owner = (core if slot < plane else 1 - core) * plane + chip
        wv32[0:3, share_lanes(slot, 1)] = wv_ref[:, pl.ds(pl.multiple_of(owner * share, 128), share)].astype(f32)
    own_waves = wv32[:, share_lanes(0, 1)]
    squared = jnp.sum(own_waves * own_waves, axis=0, keepdims=True)
    kweight = jnp.exp(-smearing * squared) / squared * scale

    def atom_phases(step):
        for part in range(8):
            rows = pl.ds(pl.multiple_of(step * 2048 + part * 256, 256), 256)
            cosines, sines = turns_cos_sin(dot_nn(wv32[:, rows].T.astype(bf16), own_coords), cos_fast, sin_fast)
            atom_phase[rows, 0:atoms] = cosines.astype(bf16)
            atom_phase[rows, atoms:2 * atoms] = sines.astype(bf16)

    atom_steps = total_k // 2048
    pl.loop(0, atom_steps // 2)(atom_phases)

    ghost_all.wait_recv()
    lane_block = lax.broadcasted_iota(jnp.int32, (8, atoms), 1) // ghosts
    ghost32 = jnp.zeros((8, atoms), f32)
    for block in range(4):
        ghost32 = jnp.where(lane_block == block, ghost_in[block].astype(f32), ghost32)
    ghost_cos, ghost_sin = turns_cos_sin(0.5 * ghost32, cos_fine, sin_fine)
    fill_pairs(pairs_ghost, ghost_counts, ghost_cos, ghost_sin)
    ghost_second = ghost32.T[:, 3:4] > 0.5
    ghost_feats = jnp.where(ghost_second, projected_kinds[1:2, :], projected_kinds[0:1, :]).astype(bf16)
    hidden = update(0, hidden, own_message + messages(0, pairs_ghost, ghost_feats))
    projected = dot_nn(hidden, win_ref[1]).astype(bf16)
    feat_out[...] = dot_nn(pick_rows, projected).astype(bf16)
    for block in (3, 2, 1, 0):
        feat_copy(block).start()
    spread_start(pos_all, p_send, p_recv)
    own_message = messages(1, pairs_own, projected)
    pl.loop(atom_steps // 2, atom_steps)(atom_phases)
    ghost_all.wait_send()
    feat_all.wait_recv()
    hidden = update(1, hidden, own_message + messages(1, pairs_ghost, feat_in[...]))
    charges = dot_nt(wch_ref[...], hidden)
    q_all[:, 0:atoms] = charges.astype(bf16)
    spread_start(q_all, q_send, q_recv)
    feat_all.wait_send()

    spread_near(pos_all, p_send, p_recv)
    spread_far(pos_all, p_send, p_recv)
    waves8 = own_waves.astype(bf16)

    def share_phases(step):
        for part in range(4):
            rows = pl.ds(pl.multiple_of(step * 512 + part * 128, 128), 128)
            places = pos_all[:, rows].astype(f32).T.astype(bf16)
            cosines, sines = turns_cos_sin(dot_nn(places, waves8), cos_fast, sin_fast)
            share_phase[rows, 0:share] = cosines.astype(bf16)
            share_phase[rows, share:2 * share] = sines.astype(bf16)

    share_steps = members * atoms // 512
    pl.loop(0, share_steps)(share_phases)
    spread_sent(pos_all, p_send, p_recv)

    near_lanes, far_lanes = slice(0, near_count * atoms), slice(near_count * atoms, members * atoms)
    spread_near(q_all, q_send, q_recv)
    both_parts = dot_nn(q_all[:, near_lanes], share_phase[near_lanes, :])
    spread_far(q_all, q_send, q_recv)
    both_parts = both_parts + dot_nn(q_all[:, far_lanes], share_phase[far_lanes, :])
    z_out[...] = (jnp.concatenate([both_parts[:, :share], both_parts[:, share:]], axis=0) * kweight).astype(bf16)
    for dz in heights:
        column_copy(dz).start()
    spread_sent(q_all, q_send, q_recv)

    column_all.wait_recv()
    summed = z_out[...].astype(f32)
    for dz in range(1, depth):
        summed = summed + z_in[dz - 1].astype(f32)
    z_full[:, share_lanes(0, 1)] = summed.astype(bf16)
    for number in range(plane - 1, 0, -1):
        plane_copy(number).start()
    twin_copy(0).start()
    column_all.wait_send()

    def apply_slots(first, last):
        for slot in range(first, last):
            lanes = share_lanes(slot, 1)
            block = z_full[:, lanes]
            left[0:16, lanes] = block
            block = block.astype(f32)
            waves = wv32[:, lanes]
            for d in range(3):
                left[16 * (d + 1):16 * (d + 2), lanes] = (block * waves[d:d + 1, :]).astype(bf16)
        lanes = share_lanes(first, last - first)
        return dot_nn(left[:, lanes], atom_phase[lanes, :])

    def take_ring(ring):
        for slot in range(max(rings[ring][0], 1), rings[ring][1]):
            plane_arrival(slot).wait_recv()
            twin_copy(slot).start()

    def take_twin_ring(ring):
        twin_arrival(ring).wait_recv()
        return apply_slots(plane + rings[ring][0], plane + rings[ring][1])

    take_ring(0)
    sums = apply_slots(*rings[0])
    take_ring(1)
    sums = sums + apply_slots(*rings[1])
    take_ring(2)
    sums = sums + take_twin_ring(0)
    sums = sums + apply_slots(*rings[2])
    sums = sums + take_twin_ring(1)
    sums = sums + take_twin_ring(2)
    plane_all.wait_send()
    by_cos, by_sin = sums[:, :atoms], sums[:, atoms:]
    out_ref[...] = jnp.zeros_like(out_ref)
    out_ref[0:latent, :] = by_cos[:latent] + by_sin[latent:2 * latent]
    for d in range(3):
        first = 2 * latent * (d + 1)
        inner = by_sin[first:first + latent] - by_cos[first + latent:first + 2 * latent]
        out_ref[latent + d:latent + d + 1, :] = jnp.sum(charges * inner, axis=0, keepdims=True)
    twin_all.wait_send()


def per_device(positions, species, neighbours, ghost_rows, wavevectors, embedding, w_in, radial, norm_gain, w_out, w_charge):
    atoms = positions.shape[1]
    total_k = wavevectors.shape[1]
    latent = w_charge.shape[1]
    channels = w_in.shape[2]
    bases = radial.shape[1]
    share = total_k // members
    scale = 1.0 / math.sqrt(atoms * lax.axis_size(("dom", "sub")))
    operands = (
        positions, species.reshape(1, atoms), ghost_rows, neighbours, wavevectors,
        embedding, w_in, radial, norm_gain, w_out, w_charge.T,
    )
    dma = pltpu.SemaphoreType.DMA
    vmem = pl.BlockSpec(memory_space=pltpu.VMEM)
    hbm = pl.BlockSpec(memory_space=pltpu.HBM)
    packed = pl.pallas_call(
        functools.partial(kernel, scale),
        out_shape=jax.ShapeDtypeStruct((16, atoms), f32),
        in_specs=[hbm] * len(operands),
        out_specs=vmem,
        scratch_shapes=[pltpu.VMEM(value.shape, value.dtype) for value in operands] + [
            pltpu.VMEM((8, atoms), f32),
            pltpu.VMEM((8, atoms), bf16),
            pltpu.VMEM((4, 8, atoms), bf16),
            pltpu.VMEM((8, atoms), f32),
            pltpu.VMEM((8, members * atoms), bf16),
            pltpu.VMEM((latent, members * atoms), bf16),
            pltpu.VMEM((8, total_k), f32),
            pltpu.VMEM((members * atoms, 2 * share), bf16),
            pltpu.VMEM((total_k, 2 * atoms), bf16),
            pltpu.VMEM((bases * atoms, 2 * atoms), bf16),
            pltpu.VMEM((bases * atoms, 2 * atoms), bf16),
            pltpu.VMEM((atoms, channels), bf16),
            pltpu.VMEM((atoms, channels), bf16),
            pltpu.VMEM((16, share), bf16),
            pltpu.VMEM((depth - 1, 16, share), bf16),
            pltpu.VMEM((16, total_k), bf16),
            pltpu.VMEM((64, total_k), bf16),
            dma((len(operands),)), dma, dma, dma, dma, dma, dma((2,)), dma, dma((2,)),
            dma, dma, dma, dma((plane,)), dma, dma((3,)),
        ],
        compiler_params=pltpu.CompilerParams(
            collective_id=0, has_side_effects=True, vmem_limit_bytes=60 * 1024 * 1024
        ),
        name="ewald_step",
    )(*operands)
    return packed[:latent], packed[latent:latent + 3]


def solution(mesh):
    return jax.shard_map(
        per_device,
        mesh=mesh,
        in_specs=(
            P(None, ("dom", "sub")),
            P(("dom", "sub")),
            P(None, ("dom", "sub")),
            P(None, ("dom", "sub")),
            P(),
            P(),
            P(),
            P(),
            P(),
            P(),
            P(),
        ),
        out_specs=(P(None, ("dom", "sub")), P(None, ("dom", "sub"))),
        check_vma=False,
    )
```

```python
import functools
import math

import jax
import jax.numpy as jnp
import numpy as np
from jax import lax
from jax.experimental import pallas as pl
from jax.experimental.pallas import tpu as pltpu
from jax.sharding import PartitionSpec as P

MESH = pl.DeviceIdType.MESH
smearing = 0.005
epsilon = 1e-05
f32 = jnp.float32
bf16 = jnp.bfloat16
side = 4
plane = side * side
members = 2 * plane
depth = 8
round_magic = 12582912.0


def fit_series(function, terms):
    nodes = (np.cos(np.pi * (np.arange(4 * terms) + 0.5) / (4 * terms)) + 1.0) / 8.0
    fitted = np.polynomial.chebyshev.Chebyshev.fit(nodes, function(np.sqrt(nodes)), terms - 1, domain=[0.0, 0.25])
    return [float(c) for c in fitted.convert(kind=np.polynomial.Polynomial).coef]


def cos_series(terms):
    return fit_series(lambda t: np.cos(2.0 * np.pi * t), terms)


def sin_series(terms):
    return fit_series(lambda t: np.sin(2.0 * np.pi * t) / t, terms)


half_sin = fit_series(lambda t: math.sqrt(2.0) * np.sin(np.pi * t) / t, 4)
half_cos = fit_series(lambda t: math.sqrt(2.0) * np.cos(np.pi * t), 4)


def horner(coefs, u):
    value = coefs[-1]
    for c in coefs[-2::-1]:
        value = value * u + c
    return value


def turns_cos_sin(turns, cos_coefs, sin_coefs):
    t = turns - ((turns + round_magic) - round_magic)
    u = t * t
    return horner(cos_coefs, u), t * horner(sin_coefs, u)


def phase_pair(turns):
    t = turns - ((turns + round_magic) - round_magic)
    u = t * t
    s = t * horner(half_sin, u)
    return 1.0 - s * s, s * horner(half_cos, u)


def dot_nt(a, b):
    return lax.dot_general(a, b, (((1,), (1,)), ((), ())), preferred_element_type=f32)


def dot_nn(a, b):
    return jnp.dot(a, b, preferred_element_type=f32)


def torus_offsets():
    every = [(dx, dy, dc) for dx in range(side) for dy in range(side) for dc in range(2)]
    return sorted(every, key=lambda o: (min(o[0], side - o[0]) + min(o[1], side - o[1]), o))


def opposite(offset):
    return (-offset[0] % side, -offset[1] % side, offset[2])


def kernel(
    scale,
    pos_hbm, spec_hbm, gr_hbm, nbr_hbm, wv_hbm, emb_hbm, win_hbm, rad_hbm, gain_hbm, wout_hbm, wch_hbm,
    out_ref,
    pos_ref, spec_ref, gr_ref, nbr_ref, wv_ref, emb_ref, win_ref, rad_ref, gain_ref, wout_ref, wch_ref,
    c32, tiles, near_coords, gpad, pos_all, q_all, wv32,
    share_phase, atom_phase, pairs_own, pairs_ghost, pairs_kind, count_out, count_in, z_out, z_in, z_full, left,
    in_sem, g1_send, g1_recv, g2_send, g2_recv, g3_send, g3_recv, p_send, p_recv, q_send, q_recv,
    zs_send, zs_recv, w_send, w_recv, x_send, x_recv,
):
    dom = lax.axis_index("dom")
    sub = lax.axis_index("sub")
    n_dom = lax.axis_size("dom")
    n_sub = lax.axis_size("sub")
    zl, xy = dom // plane, lax.rem(dom, plane)
    my_x, my_y = xy // side, lax.rem(xy, side)
    zh, core = sub // 2, lax.rem(sub, 2)
    z_me = zh * (depth // 2) + zl
    atoms = pos_ref.shape[1]
    total_k = wv_ref.shape[1]
    share = total_k // members
    latent = wch_ref.shape[0]
    bases = rad_ref.shape[1]
    ghosts = gr_ref.shape[1]

    def member(offset):
        dx, dy, dc = offset
        chip = lax.rem(my_x + dx, side) * side + lax.rem(my_y + dy, side)
        return (zl * plane + chip, zh * 2 + (1 - core if dc else core))

    def column_member(dz):
        index = lax.rem(z_me + dz, depth)
        return (lax.rem(index, depth // 2) * plane + xy, (index // (depth // 2)) * 2 + core)

    steps = ((-1, 0), (1, 0), (0, -1), (0, 1))
    around = ((0, -1), (0, 1), (-1, -1), (-1, 1), (1, -1), (1, 1), (0, 2), (-1, 0), (1, 0), (-2, 0), (2, 0))

    def place(step):
        return (step[0], step[1] % 4)

    def beside(step):
        return (lax.rem(dom + step[0] + n_dom, n_dom), lax.rem(sub + step[1] + n_sub, n_sub))

    def reverse(step):
        return (-step[0], -step[1])

    tile_of = {place(step): number for number, step in enumerate(around)}
    tile_of[(0, 0)] = len(around)
    neighbours_at = tuple(beside(reverse(step)) for step in steps)
    offsets = torus_offsets()
    slot_of = {offset: slot for slot, offset in enumerate(offsets)}
    chip_offsets = [offset for offset in offsets if offset[2] == 0]
    heights = sorted(range(1, depth), key=lambda dz: -min(dz, depth - dz))

    fetches = [
        pltpu.make_async_copy(source, target, in_sem.at[number])
        for number, (source, target) in enumerate((
            (pos_hbm, pos_ref), (spec_hbm, spec_ref), (gr_hbm, gr_ref), (nbr_hbm, nbr_ref), (wv_hbm, wv_ref),
            (emb_hbm, emb_ref), (win_hbm, win_ref), (rad_hbm, rad_ref), (gain_hbm, gain_ref), (wout_hbm, wout_ref),
            (wch_hbm, wch_ref)))
    ]
    barrier = pltpu.get_barrier_semaphore()

    def greet(target):
        pl.semaphore_signal(barrier, inc=1, device_id=target, device_id_type=MESH)

    for step in around:
        greet(beside(step))
    for fetch in fetches[:3]:
        fetch.start()
    for offset in offsets[:0:-1]:
        greet(member(offset))
    for dz in heights:
        greet(column_member(dz))
    for fetch in fetches[3:]:
        fetch.start()

    c32[...] = jnp.zeros_like(c32)
    gpad[...] = jnp.zeros_like(gpad)
    for fetch in fetches[:3]:
        fetch.wait()
    c32[0:3, :] = pos_ref[...].astype(f32)
    c32[3:4, :] = spec_ref[...].astype(f32)
    own32 = c32[...]
    own_coords = own32.astype(bf16)
    gpad[0:4, 0:ghosts] = gr_ref[...].astype(f32)
    grown = gpad[...]
    picks = grown[1:2, :]
    for block, source in ((1, 0), (2, 3), (3, 2)):
        picks = picks + pltpu.roll(grown, block * ghosts, axis=1)[source:source + 1, :]
    row_number = lax.broadcasted_iota(jnp.int32, (atoms, atoms), 0).astype(f32)
    pick_cols = jnp.where(row_number == picks, 1.0, 0.0)
    pick_cols = pick_cols.astype(bf16)
    tiles[len(around)] = dot_nn(own_coords, pick_cols).astype(bf16)
    pos_all[:, 0:atoms] = own_coords

    def tile_copy(step):
        return pltpu.make_async_remote_copy(
            src_ref=tiles.at[len(around)], dst_ref=tiles.at[tile_of[place(reverse(step))]], send_sem=g1_send,
            recv_sem=g1_recv, device_id=beside(step), device_id_type=MESH)

    def near_copy(block):
        return pltpu.make_async_remote_copy(
            src_ref=pos_all.at[:, pl.ds(0, atoms)], dst_ref=near_coords.at[block], send_sem=g2_send, recv_sem=g2_recv,
            device_id=neighbours_at[block], device_id_type=MESH)

    def count_copy(block):
        rows = pl.ds(block * ghosts, ghosts)
        return pltpu.make_async_remote_copy(
            src_ref=count_out.at[rows], dst_ref=count_in.at[rows], send_sem=g3_send, recv_sem=g3_recv,
            device_id=neighbours_at[block], device_id_type=MESH)

    def slot_lanes(first, count):
        return pl.ds(first * atoms, count * atoms)

    near_count = members // 2

    def spread_copy(buffer, send, recv, offset):
        landing = slot_of[opposite(offset)]
        return pltpu.make_async_remote_copy(
            src_ref=buffer.at[:, slot_lanes(0, 1)], dst_ref=buffer.at[:, slot_lanes(landing, 1)],
            send_sem=send, recv_sem=recv.at[0 if landing < near_count else 1],
            device_id=member(offset), device_id_type=MESH)

    def spread_all(buffer, send, recv, first, count, group):
        lanes = slot_lanes(first, count)
        return pltpu.make_async_remote_copy(
            src_ref=buffer.at[:, lanes], dst_ref=buffer.at[:, lanes], send_sem=send, recv_sem=recv.at[group],
            device_id=member(offsets[1]), device_id_type=MESH)

    def spread_start(buffer, send, recv):
        for offset in offsets[:0:-1]:
            spread_copy(buffer, send, recv, offset).start()

    def spread_near(buffer, send, recv):
        spread_all(buffer, send, recv, 1, near_count - 1, 0).wait_recv()

    def spread_far(buffer, send, recv):
        spread_all(buffer, send, recv, near_count, members - near_count, 1).wait_recv()

    def spread_sent(buffer, send, recv):
        spread_all(buffer, send, recv, 1, members - 1, 0).wait_send()

    def column_copy(dz):
        return pltpu.make_async_remote_copy(
            src_ref=z_out, dst_ref=z_in.at[dz - 1], send_sem=zs_send, recv_sem=zs_recv,
            device_id=column_member(dz), device_id_type=MESH)

    column_all = pltpu.make_async_remote_copy(
        src_ref=z_in, dst_ref=z_in, send_sem=zs_send, recv_sem=zs_recv,
        device_id=column_member(1), device_id_type=MESH)

    def share_lanes(first, count):
        return pl.ds(first * share, count * share)

    def plane_copy(number):
        landing = chip_offsets.index(opposite(chip_offsets[number]))
        return pltpu.make_async_remote_copy(
            src_ref=z_full.at[:, share_lanes(0, 1)], dst_ref=z_full.at[:, share_lanes(landing, 1)],
            send_sem=w_send, recv_sem=w_recv.at[landing], device_id=member(chip_offsets[number]), device_id_type=MESH)

    def plane_arrival(slot):
        lanes = share_lanes(slot, 1)
        return pltpu.make_async_remote_copy(
            src_ref=z_full.at[:, lanes], dst_ref=z_full.at[:, lanes], send_sem=w_send, recv_sem=w_recv.at[slot],
            device_id=member(chip_offsets[1]), device_id_type=MESH)

    plane_all = pltpu.make_async_remote_copy(
        src_ref=z_full.at[:, share_lanes(1, plane - 1)], dst_ref=z_full.at[:, share_lanes(1, plane - 1)],
        send_sem=w_send, recv_sem=w_recv.at[0], device_id=member(chip_offsets[1]), device_id_type=MESH)
    twin = (dom, zh * 2 + 1 - core)
    rings = ((0, 5), (5, 11), (11, plane))

    def twin_copy(slot):
        ring = [first <= slot < last for first, last in rings].index(True)
        return pltpu.make_async_remote_copy(
            src_ref=z_full.at[:, share_lanes(slot, 1)], dst_ref=z_full.at[:, share_lanes(plane + slot, 1)],
            send_sem=x_send, recv_sem=x_recv.at[ring], device_id=twin, device_id_type=MESH)

    def twin_arrival(ring):
        first, last = rings[ring]
        lanes = share_lanes(plane + first, last - first)
        return pltpu.make_async_remote_copy(
            src_ref=z_full.at[:, lanes], dst_ref=z_full.at[:, lanes], send_sem=x_send, recv_sem=x_recv.at[ring],
            device_id=twin, device_id_type=MESH)

    twin_all = pltpu.make_async_remote_copy(
        src_ref=z_full.at[:, share_lanes(0, plane)], dst_ref=z_full.at[:, share_lanes(0, plane)],
        send_sem=x_send, recv_sem=x_recv.at[0], device_id=twin, device_id_type=MESH)
    tiles_all = pltpu.make_async_remote_copy(
        src_ref=tiles.at[pl.ds(0, len(around))], dst_ref=tiles.at[pl.ds(0, len(around))], send_sem=g1_send,
        recv_sem=g1_recv, device_id=twin, device_id_type=MESH)
    near_all = pltpu.make_async_remote_copy(
        src_ref=near_coords, dst_ref=near_coords, send_sem=g2_send, recv_sem=g2_recv, device_id=twin, device_id_type=MESH)
    count_all = pltpu.make_async_remote_copy(
        src_ref=count_in, dst_ref=count_in, send_sem=g3_send, recv_sem=g3_recv, device_id=twin, device_id_type=MESH)

    pl.semaphore_wait(barrier, len(around) + (members - 1) + (depth - 1))
    for step in around:
        tile_copy(step).start()
    for block in (3, 2, 1, 0):
        near_copy(block).start()

    for fetch in fetches[3:]:
        fetch.wait()
    listed = nbr_ref[...]
    quarters = []
    for first in range(0, 2 * atoms, 64):
        table_row = lax.broadcasted_iota(jnp.int32, (64, atoms), 0) + first
        counted = jnp.zeros((64, atoms), f32)
        for slot in range(listed.shape[0]):
            counted = jnp.where(table_row == listed[slot:slot + 1, :], counted + 1.0, counted)
        quarters.append(counted)
    own_counts_t, ghost_counts_t = jnp.concatenate(quarters[:2], axis=0), jnp.concatenate(quarters[2:], axis=0)
    count_out[:, 0:atoms] = dot_nn(own_counts_t.astype(bf16), pick_cols).T.astype(bf16)
    count_out[:, atoms:2 * atoms] = dot_nn(ghost_counts_t.astype(bf16), pick_cols).T.astype(bf16)
    for block in (3, 2, 1, 0):
        count_copy(block).start()
    spread_start(pos_all, p_send, p_recv)
    own_counts, ghost_counts = own_counts_t.T, ghost_counts_t.T

    cos_fine, sin_fine = cos_series(9), sin_series(9)
    own_cos, own_sin = turns_cos_sin(0.5 * own32, cos_fine, sin_fine)
    own_cos_col, own_sin_col = own_cos.T, own_sin.T
    embedding = emb_ref[...].astype(f32)
    gains = gain_ref[...].astype(f32)
    is_second = own32.T[:, 3:4] > 0.5
    hidden = jnp.where(is_second, embedding[1:2, :], embedding[0:1, :])
    both = lax.broadcasted_iota(jnp.int32, (16, embedding.shape[1]), 0)
    both = jnp.where(both == 1, embedding[1:2, :], embedding[0:1, :]).astype(bf16)
    projected_kinds = dot_nn(both, win_ref[0]).astype(bf16).astype(f32)
    own_feats = jnp.where(is_second, projected_kinds[1:2, :], projected_kinds[0:1, :]).astype(bf16)

    def fill_pairs(pairs, counts, table_cos, table_sin):
        chord = jnp.zeros((atoms, atoms), f32)
        for d in range(3):
            apart = table_sin[d:d + 1, :] * own_cos_col[:, d:d + 1] - table_cos[d:d + 1, :] * own_sin_col[:, d:d + 1]
            chord = chord + apart * apart
        basis = jnp.exp(-0.125 * chord)
        for b in range(bases):
            pair = counts * basis
            high = pair.astype(bf16)
            rows = slice(b * atoms, (b + 1) * atoms)
            pairs[rows, 0:atoms] = high
            pairs[rows, atoms:2 * atoms] = (pair - high.astype(f32)).astype(bf16)
            basis = basis * basis

    def messages(number, pairs, feats):
        return radial_sum(number, dot_nn(pairs[...], jnp.concatenate([feats, feats], axis=0)))

    def radial_sum(number, products):
        radial_layer = rad_ref[number].astype(f32)
        message = radial_layer[0:1, :] * products[:atoms]
        for b in range(1, bases):
            message = message + radial_layer[b:b + 1, :] * products[b * atoms:(b + 1) * atoms]
        return message

    def update(number, hidden, message):
        normed = message * lax.rsqrt(jnp.mean(message * message, axis=1, keepdims=True) + epsilon)
        normed = normed * gains[number:number + 1, :]
        activated = (normed / (1.0 + jnp.exp(-normed))).astype(bf16)
        return (hidden + dot_nn(activated, wout_ref[number])).astype(bf16)

    fill_pairs(pairs_own, own_counts, own_cos, own_sin)
    own_message = messages(0, pairs_own, own_feats)

    wv32[...] = jnp.zeros_like(wv32)
    for slot in range(members):
        dx, dy, _ = chip_offsets[slot % plane]
        chip = lax.rem(my_x + dx, side) * side + lax.rem(my_y + dy, side)
        owner = (core if slot < plane else 1 - core) * plane + chip
        wv32[0:3, share_lanes(slot, 1)] = wv_ref[:, pl.ds(pl.multiple_of(owner * share, 128), share)].astype(f32)
    own_waves = wv32[:, share_lanes(0, 1)]
    waves8 = own_waves.astype(bf16)

    def share_phases(step):
        for part in range(8):
            rows = pl.ds(pl.multiple_of(step * 1024 + part * 128, 128), 128)
            places = pos_all[:, rows].astype(f32).T.astype(bf16)
            cosines, sines = phase_pair(dot_nn(places, waves8))
            share_phase[rows, 0:share] = cosines.astype(bf16)
            share_phase[rows, share:2 * share] = sines.astype(bf16)

    def atom_phases(step):
        for part in range(8):
            rows = pl.ds(pl.multiple_of(step * 2048 + part * 256, 256), 256)
            cosines, sines = phase_pair(dot_nn(wv32[:, rows].T.astype(bf16), own_coords))
            atom_phase[rows, 0:atoms] = cosines.astype(bf16)
            atom_phase[rows, atoms:2 * atoms] = sines.astype(bf16)

    squared = jnp.sum(own_waves * own_waves, axis=0, keepdims=True)
    kweight = jnp.exp(-smearing * squared) / squared * scale

    pl.loop(0, 2)(atom_phases)
    tiles_all.wait_recv()
    near_all.wait_recv()
    lane_block = lax.broadcasted_iota(jnp.int32, (8, atoms), 1) // ghosts

    def ghosts_of(step):
        merged = jnp.zeros((8, atoms), f32)
        for block in range(4):
            source = place((step[0] + steps[block][0], step[1] + steps[block][1]))
            merged = jnp.where(lane_block == block, tiles[tile_of[source]].astype(f32), merged)
        return merged

    ghost32 = ghosts_of((0, 0))
    tables = [ghost32] + [near_coords[block].astype(f32) for block in range(4)] + [ghosts_of(step) for step in steps]
    table_cos, table_sin = turns_cos_sin(0.5 * jnp.concatenate(tables, axis=0), cos_fine, sin_fine)
    ghost_cos, ghost_sin = table_cos[0:8], table_sin[0:8]
    fill_pairs(pairs_ghost, ghost_counts, ghost_cos, ghost_sin)
    ghost_second = ghost32.T[:, 3:4] > 0.5
    ghost_feats = jnp.where(ghost_second, projected_kinds[1:2, :], projected_kinds[0:1, :]).astype(bf16)

    ghost_cos_col, ghost_sin_col = ghost_cos.T, ghost_sin.T
    count_all.wait_recv()
    halves = []
    for half in range(2):
        chords, kinds = [], []
        for block in range(4):
            entry = 1 + half * 4 + block
            rows = slice(block * ghosts, (block + 1) * ghosts)
            chord = jnp.zeros((ghosts, atoms), f32)
            for d in range(3):
                at = entry * 8 + d
                apart = table_sin[at:at + 1, :] * ghost_cos_col[rows, d:d + 1] - table_cos[at:at + 1, :] * ghost_sin_col[rows, d:d + 1]
                chord = chord + apart * apart
            chords.append(chord)
            kinds.append(jnp.broadcast_to(tables[entry][3:4, :], (ghosts, atoms)))
        basis = jnp.exp(-0.125 * jnp.concatenate(chords, axis=0))
        halves.append([basis, count_in[:, half * atoms:(half + 1) * atoms].astype(f32), jnp.concatenate(kinds, axis=0)])
    for b in range(bases):
        pair0, pair1 = (basis * counts for basis, counts, _ in halves)
        second = pair0 * halves[0][2] + pair1 * halves[1][2]
        first = pair0 + pair1 - second
        rows = slice(b * atoms, (b + 1) * atoms)
        for number, part in enumerate((first, second)):
            high = part.astype(bf16)
            pairs_kind[rows, 2 * number * atoms:(2 * number + 1) * atoms] = high
            pairs_kind[rows, (2 * number + 1) * atoms:(2 * number + 2) * atoms] = (part - high.astype(f32)).astype(bf16)
        for half in halves:
            half[0] = half[0] * half[0]
    kind_rows = jnp.concatenate(
        [jnp.broadcast_to(projected_kinds[kind:kind + 1, :], (2 * atoms, projected_kinds.shape[1])) for kind in range(2)],
        axis=0).astype(bf16)
    ghost_message = radial_sum(0, dot_nn(pairs_kind[...], kind_rows))
    message = jnp.concatenate([own_message + messages(0, pairs_ghost, ghost_feats), ghost_message], axis=0)
    ghost_hidden = jnp.where(ghost_second, embedding[1:2, :], embedding[0:1, :])
    everyone = update(0, jnp.concatenate([hidden, ghost_hidden], axis=0), message)
    hidden = everyone[:atoms]
    projected = dot_nn(everyone, win_ref[1]).astype(bf16)
    message = messages(1, pairs_own, projected[:atoms]) + messages(1, pairs_ghost, projected[atoms:])
    hidden = update(1, hidden, message)
    charges = dot_nt(wch_ref[...], hidden)
    q_all[:, 0:atoms] = charges.astype(bf16)
    spread_start(q_all, q_send, q_recv)
    tiles_all.wait_send()
    near_all.wait_send()
    count_all.wait_send()

    spread_near(pos_all, p_send, p_recv)
    spread_far(pos_all, p_send, p_recv)
    pl.loop(0, 4)(share_phases)
    spread_sent(pos_all, p_send, p_recv)

    near_lanes, far_lanes = slice(0, near_count * atoms), slice(near_count * atoms, members * atoms)
    spread_near(q_all, q_send, q_recv)
    both_parts = dot_nn(q_all[:, near_lanes], share_phase[near_lanes, :])
    spread_far(q_all, q_send, q_recv)
    both_parts = both_parts + dot_nn(q_all[:, far_lanes], share_phase[far_lanes, :])
    z_out[...] = (jnp.concatenate([both_parts[:, :share], both_parts[:, share:]], axis=0) * kweight).astype(bf16)
    for dz in heights:
        column_copy(dz).start()
    pl.loop(2, 6)(atom_phases)
    spread_sent(q_all, q_send, q_recv)

    column_all.wait_recv()
    summed = z_out[...].astype(f32)
    for dz in range(1, depth):
        summed = summed + z_in[dz - 1].astype(f32)
    z_full[:, share_lanes(0, 1)] = summed.astype(bf16)
    for number in range(plane - 1, 0, -1):
        plane_copy(number).start()
    twin_copy(0).start()
    column_all.wait_send()

    def apply_slots(first, last):
        for slot in range(first, last):
            lanes = share_lanes(slot, 1)
            block = z_full[:, lanes]
            left[0:16, lanes] = block
            block = block.astype(f32)
            waves = wv32[:, lanes]
            for d in range(3):
                left[16 * (d + 1):16 * (d + 2), lanes] = (block * waves[d:d + 1, :]).astype(bf16)
        lanes = share_lanes(first, last - first)
        return dot_nn(left[:, lanes], atom_phase[lanes, :])

    def take_ring(ring):
        for slot in range(max(rings[ring][0], 1), rings[ring][1]):
            plane_arrival(slot).wait_recv()
            twin_copy(slot).start()

    def take_twin_ring(ring):
        twin_arrival(ring).wait_recv()
        return apply_slots(plane + rings[ring][0], plane + rings[ring][1])

    take_ring(0)
    sums = apply_slots(*rings[0])
    take_ring(1)
    sums = sums + apply_slots(*rings[1])
    take_ring(2)
    sums = sums + take_twin_ring(0)
    sums = sums + apply_slots(*rings[2])
    sums = sums + take_twin_ring(1)
    sums = sums + take_twin_ring(2)
    plane_all.wait_send()
    by_cos, by_sin = sums[:, :atoms], sums[:, atoms:]
    out_ref[...] = jnp.zeros_like(out_ref)
    out_ref[0:latent, :] = by_cos[:latent] + by_sin[latent:2 * latent]
    for d in range(3):
        first = 2 * latent * (d + 1)
        inner = by_sin[first:first + latent] - by_cos[first + latent:first + 2 * latent]
        out_ref[latent + d:latent + d + 1, :] = jnp.sum(charges * inner, axis=0, keepdims=True)
    twin_all.wait_send()


def per_device(positions, species, neighbours, ghost_rows, wavevectors, embedding, w_in, radial, norm_gain, w_out, w_charge):
    atoms = positions.shape[1]
    total_k = wavevectors.shape[1]
    latent = w_charge.shape[1]
    bases = radial.shape[1]
    share = total_k // members
    scale = 1.0 / math.sqrt(atoms * lax.axis_size(("dom", "sub")))
    operands = (
        positions, species.reshape(1, atoms), ghost_rows, neighbours, wavevectors,
        embedding, w_in, radial, norm_gain, w_out, w_charge.T,
    )
    dma = pltpu.SemaphoreType.DMA
    vmem = pl.BlockSpec(memory_space=pltpu.VMEM)
    hbm = pl.BlockSpec(memory_space=pltpu.HBM)
    packed = pl.pallas_call(
        functools.partial(kernel, scale),
        out_shape=jax.ShapeDtypeStruct((16, atoms), f32),
        in_specs=[hbm] * len(operands),
        out_specs=vmem,
        scratch_shapes=[pltpu.VMEM(value.shape, value.dtype) for value in operands] + [
            pltpu.VMEM((8, atoms), f32),
            pltpu.VMEM((12, 8, atoms), bf16),
            pltpu.VMEM((4, 8, atoms), bf16),
            pltpu.VMEM((8, atoms), f32),
            pltpu.VMEM((8, members * atoms), bf16),
            pltpu.VMEM((latent, members * atoms), bf16),
            pltpu.VMEM((8, total_k), f32),
            pltpu.VMEM((members * atoms, 2 * share), bf16),
            pltpu.VMEM((total_k, 2 * atoms), bf16),
            pltpu.VMEM((bases * atoms, 2 * atoms), bf16),
            pltpu.VMEM((bases * atoms, 2 * atoms), bf16),
            pltpu.VMEM((bases * atoms, 4 * atoms), bf16),
            pltpu.VMEM((atoms, 2 * atoms), bf16),
            pltpu.VMEM((atoms, 2 * atoms), bf16),
            pltpu.VMEM((16, share), bf16),
            pltpu.VMEM((depth - 1, 16, share), bf16),
            pltpu.VMEM((16, total_k), bf16),
            pltpu.VMEM((64, total_k), bf16),
            dma((len(operands),)), dma, dma, dma, dma, dma, dma, dma, dma((2,)), dma, dma((2,)),
            dma, dma, dma, dma((plane,)), dma, dma((3,)),
        ],
        compiler_params=pltpu.CompilerParams(
            collective_id=0, has_side_effects=True, vmem_limit_bytes=60 * 1024 * 1024
        ),
        name="ewald_step",
    )(*operands)
    return packed[:latent], packed[latent:latent + 3]


def solution(mesh):
    return jax.shard_map(
        per_device,
        mesh=mesh,
        in_specs=(
            P(None, ("dom", "sub")),
            P(("dom", "sub")),
            P(None, ("dom", "sub")),
            P(None, ("dom", "sub")),
            P(),
            P(),
            P(),
            P(),
            P(),
            P(),
            P(),
        ),
        out_specs=(P(None, ("dom", "sub")), P(None, ("dom", "sub"))),
        check_vma=False,
    )
```

```python
import functools
import math

import jax
import jax.numpy as jnp
import numpy as np
from jax import lax
from jax.experimental import pallas as pl
from jax.experimental.pallas import tpu as pltpu
from jax.sharding import PartitionSpec as P

MESH = pl.DeviceIdType.MESH
smearing = 0.005
epsilon = 1e-05
f32 = jnp.float32
bf16 = jnp.bfloat16
side = 4
plane = side * side
members = 2 * plane
depth = 8
round_magic = 12582912.0


def fit_series(function, terms):
    nodes = (np.cos(np.pi * (np.arange(4 * terms) + 0.5) / (4 * terms)) + 1.0) / 8.0
    fitted = np.polynomial.chebyshev.Chebyshev.fit(nodes, function(np.sqrt(nodes)), terms - 1, domain=[0.0, 0.25])
    return [float(c) for c in fitted.convert(kind=np.polynomial.Polynomial).coef]


def cos_series(terms):
    return fit_series(lambda t: np.cos(2.0 * np.pi * t), terms)


def sin_series(terms):
    return fit_series(lambda t: np.sin(2.0 * np.pi * t) / t, terms)


half_sin = fit_series(lambda t: math.sqrt(2.0) * np.sin(np.pi * t) / t, 4)
half_cos = fit_series(lambda t: math.sqrt(2.0) * np.cos(np.pi * t), 4)


def horner(coefs, u):
    value = coefs[-1]
    for c in coefs[-2::-1]:
        value = value * u + c
    return value


def turns_cos_sin(turns, cos_coefs, sin_coefs):
    t = turns - ((turns + round_magic) - round_magic)
    u = t * t
    return horner(cos_coefs, u), t * horner(sin_coefs, u)


def phase_pair(turns):
    t = turns - ((turns + round_magic) - round_magic)
    u = t * t
    s = t * horner(half_sin, u)
    return 1.0 - s * s, s * horner(half_cos, u)


def dot_nt(a, b):
    return lax.dot_general(a, b, (((1,), (1,)), ((), ())), preferred_element_type=f32)


def dot_nn(a, b):
    return jnp.dot(a, b, preferred_element_type=f32)


def torus_offsets():
    every = [(dx, dy, dc) for dx in range(side) for dy in range(side) for dc in range(2)]
    return sorted(every, key=lambda o: (min(o[0], side - o[0]) + min(o[1], side - o[1]), o))


def opposite(offset):
    return (-offset[0] % side, -offset[1] % side, offset[2])


def kernel(
    scale,
    pos_hbm, spec_hbm, gr_hbm, nbr_hbm, wv_hbm, emb_hbm, win_hbm, rad_hbm, gain_hbm, wout_hbm, wch_hbm,
    pot_ref, force_ref,
    pos_ref, spec_ref, gr_ref, nbr_ref, wv_ref, emb_ref, win_ref, rad_ref, gain_ref, wout_ref, wch_ref,
    c32, tiles, near_coords, gpad, pos_all, q_all, wv32,
    share_phase, atom_phase, pairs_own, pairs_ghost, pairs_kind, count_out, count_in, z_out, z_in, z_full, left,
    in_sem, g1_send, g1_recv, g2_send, g2_recv, g3_send, g3_recv, p_send, p_recv, q_send, q_recv,
    zs_send, zs_recv, w_send, w_recv, x_send, x_recv,
):
    dom = lax.axis_index("dom")
    sub = lax.axis_index("sub")
    n_dom = lax.axis_size("dom")
    n_sub = lax.axis_size("sub")
    zl, xy = dom // plane, lax.rem(dom, plane)
    my_x, my_y = xy // side, lax.rem(xy, side)
    zh, core = sub // 2, lax.rem(sub, 2)
    z_me = zh * (depth // 2) + zl
    atoms = pos_ref.shape[1]
    total_k = wv_ref.shape[1]
    share = total_k // members
    latent = wch_ref.shape[0]
    bases = rad_ref.shape[1]
    ghosts = gr_ref.shape[1]

    def member(offset):
        dx, dy, dc = offset
        chip = lax.rem(my_x + dx, side) * side + lax.rem(my_y + dy, side)
        return (zl * plane + chip, zh * 2 + (1 - core if dc else core))

    def column_member(dz):
        index = lax.rem(z_me + dz, depth)
        return (lax.rem(index, depth // 2) * plane + xy, (index // (depth // 2)) * 2 + core)

    steps = ((-1, 0), (1, 0), (0, -1), (0, 1))
    around = ((0, -1), (0, 1), (-1, -1), (-1, 1), (1, -1), (1, 1), (0, 2), (-1, 0), (1, 0), (-2, 0), (2, 0))

    def place(step):
        return (step[0], step[1] % 4)

    def beside(step):
        return (lax.rem(dom + step[0] + n_dom, n_dom), lax.rem(sub + step[1] + n_sub, n_sub))

    def reverse(step):
        return (-step[0], -step[1])

    tile_of = {place(step): number for number, step in enumerate(around)}
    tile_of[(0, 0)] = len(around)
    neighbours_at = tuple(beside(reverse(step)) for step in steps)
    offsets = torus_offsets()
    slot_of = {offset: slot for slot, offset in enumerate(offsets)}
    chip_offsets = [offset for offset in offsets if offset[2] == 0]
    heights = sorted(range(1, depth), key=lambda dz: -min(dz, depth - dz))

    fetches = [
        pltpu.make_async_copy(source, target, in_sem.at[number])
        for number, (source, target) in enumerate((
            (pos_hbm, pos_ref), (spec_hbm, spec_ref), (gr_hbm, gr_ref), (nbr_hbm, nbr_ref), (wv_hbm, wv_ref),
            (emb_hbm, emb_ref), (win_hbm, win_ref), (rad_hbm, rad_ref), (gain_hbm, gain_ref), (wout_hbm, wout_ref),
            (wch_hbm, wch_ref)))
    ]
    barrier = pltpu.get_barrier_semaphore()

    def greet(target):
        pl.semaphore_signal(barrier, inc=1, device_id=target, device_id_type=MESH)

    for step in around:
        greet(beside(step))
    for fetch in fetches[:3]:
        fetch.start()
    for offset in offsets[:0:-1]:
        greet(member(offset))
    for dz in heights:
        greet(column_member(dz))
    for fetch in fetches[3:]:
        fetch.start()

    c32[...] = jnp.zeros_like(c32)
    gpad[...] = jnp.zeros_like(gpad)
    for fetch in fetches[:3]:
        fetch.wait()
    c32[0:3, :] = pos_ref[...].astype(f32)
    c32[3:4, :] = spec_ref[...].astype(f32)
    own32 = c32[...]
    own_coords = own32.astype(bf16)
    gpad[0:4, 0:ghosts] = gr_ref[...].astype(f32)
    grown = gpad[...]
    picks = grown[1:2, :]
    for block, source in ((1, 0), (2, 3), (3, 2)):
        picks = picks + pltpu.roll(grown, block * ghosts, axis=1)[source:source + 1, :]
    row_number = lax.broadcasted_iota(jnp.int32, (atoms, atoms), 0).astype(f32)
    pick_cols = jnp.where(row_number == picks, 1.0, 0.0)
    pick_cols = pick_cols.astype(bf16)
    tiles[len(around)] = dot_nn(own_coords, pick_cols).astype(bf16)
    pos_all[:, 0:atoms] = own_coords

    def tile_copy(step):
        return pltpu.make_async_remote_copy(
            src_ref=tiles.at[len(around)], dst_ref=tiles.at[tile_of[place(reverse(step))]], send_sem=g1_send,
            recv_sem=g1_recv, device_id=beside(step), device_id_type=MESH)

    def near_copy(block):
        return pltpu.make_async_remote_copy(
            src_ref=pos_all.at[:, pl.ds(0, atoms)], dst_ref=near_coords.at[block], send_sem=g2_send, recv_sem=g2_recv,
            device_id=neighbours_at[block], device_id_type=MESH)

    def count_copy(block):
        rows = pl.ds(block * ghosts, ghosts)
        return pltpu.make_async_remote_copy(
            src_ref=count_out.at[rows], dst_ref=count_in.at[rows], send_sem=g3_send, recv_sem=g3_recv,
            device_id=neighbours_at[block], device_id_type=MESH)

    def slot_lanes(first, count):
        return pl.ds(first * atoms, count * atoms)

    near_count = members // 2

    def spread_copy(buffer, send, recv, offset):
        landing = slot_of[opposite(offset)]
        return pltpu.make_async_remote_copy(
            src_ref=buffer.at[:, slot_lanes(0, 1)], dst_ref=buffer.at[:, slot_lanes(landing, 1)],
            send_sem=send, recv_sem=recv.at[0 if landing < near_count else 1],
            device_id=member(offset), device_id_type=MESH)

    def spread_all(buffer, send, recv, first, count, group):
        lanes = slot_lanes(first, count)
        return pltpu.make_async_remote_copy(
            src_ref=buffer.at[:, lanes], dst_ref=buffer.at[:, lanes], send_sem=send, recv_sem=recv.at[group],
            device_id=member(offsets[1]), device_id_type=MESH)

    def spread_start(buffer, send, recv):
        for offset in offsets[:0:-1]:
            spread_copy(buffer, send, recv, offset).start()

    def spread_near(buffer, send, recv):
        spread_all(buffer, send, recv, 1, near_count - 1, 0).wait_recv()

    def spread_far(buffer, send, recv):
        spread_all(buffer, send, recv, near_count, members - near_count, 1).wait_recv()

    def spread_sent(buffer, send, recv):
        spread_all(buffer, send, recv, 1, members - 1, 0).wait_send()

    def column_copy(dz):
        return pltpu.make_async_remote_copy(
            src_ref=z_out, dst_ref=z_in.at[dz - 1], send_sem=zs_send, recv_sem=zs_recv,
            device_id=column_member(dz), device_id_type=MESH)

    column_all = pltpu.make_async_remote_copy(
        src_ref=z_in, dst_ref=z_in, send_sem=zs_send, recv_sem=zs_recv,
        device_id=column_member(1), device_id_type=MESH)

    def share_lanes(first, count):
        return pl.ds(first * share, count * share)

    def plane_copy(number):
        landing = chip_offsets.index(opposite(chip_offsets[number]))
        return pltpu.make_async_remote_copy(
            src_ref=z_full.at[:, share_lanes(0, 1)], dst_ref=z_full.at[:, share_lanes(landing, 1)],
            send_sem=w_send, recv_sem=w_recv.at[landing], device_id=member(chip_offsets[number]), device_id_type=MESH)

    def plane_arrival(slot):
        lanes = share_lanes(slot, 1)
        return pltpu.make_async_remote_copy(
            src_ref=z_full.at[:, lanes], dst_ref=z_full.at[:, lanes], send_sem=w_send, recv_sem=w_recv.at[slot],
            device_id=member(chip_offsets[1]), device_id_type=MESH)

    plane_all = pltpu.make_async_remote_copy(
        src_ref=z_full.at[:, share_lanes(1, plane - 1)], dst_ref=z_full.at[:, share_lanes(1, plane - 1)],
        send_sem=w_send, recv_sem=w_recv.at[0], device_id=member(chip_offsets[1]), device_id_type=MESH)
    twin = (dom, zh * 2 + 1 - core)
    rings = ((0, 5), (5, 11), (11, plane))

    def twin_copy(slot):
        ring = [first <= slot < last for first, last in rings].index(True)
        return pltpu.make_async_remote_copy(
            src_ref=z_full.at[:, share_lanes(slot, 1)], dst_ref=z_full.at[:, share_lanes(plane + slot, 1)],
            send_sem=x_send, recv_sem=x_recv.at[ring], device_id=twin, device_id_type=MESH)

    def twin_arrival(ring):
        first, last = rings[ring]
        lanes = share_lanes(plane + first, last - first)
        return pltpu.make_async_remote_copy(
            src_ref=z_full.at[:, lanes], dst_ref=z_full.at[:, lanes], send_sem=x_send, recv_sem=x_recv.at[ring],
            device_id=twin, device_id_type=MESH)

    twin_all = pltpu.make_async_remote_copy(
        src_ref=z_full.at[:, share_lanes(0, plane)], dst_ref=z_full.at[:, share_lanes(0, plane)],
        send_sem=x_send, recv_sem=x_recv.at[0], device_id=twin, device_id_type=MESH)
    tiles_all = pltpu.make_async_remote_copy(
        src_ref=tiles.at[pl.ds(0, len(around))], dst_ref=tiles.at[pl.ds(0, len(around))], send_sem=g1_send,
        recv_sem=g1_recv, device_id=twin, device_id_type=MESH)
    near_all = pltpu.make_async_remote_copy(
        src_ref=near_coords, dst_ref=near_coords, send_sem=g2_send, recv_sem=g2_recv, device_id=twin, device_id_type=MESH)
    count_all = pltpu.make_async_remote_copy(
        src_ref=count_in, dst_ref=count_in, send_sem=g3_send, recv_sem=g3_recv, device_id=twin, device_id_type=MESH)

    pl.semaphore_wait(barrier, len(around) + (members - 1) + (depth - 1))
    for step in around:
        tile_copy(step).start()
    for block in (3, 2, 1, 0):
        near_copy(block).start()

    for fetch in fetches[3:]:
        fetch.wait()
    listed = nbr_ref[...]
    quarters = []
    for first in range(0, 2 * atoms, 64):
        table_row = lax.broadcasted_iota(jnp.int32, (64, atoms), 0) + first
        counted = jnp.zeros((64, atoms), f32)
        for slot in range(listed.shape[0]):
            counted = jnp.where(table_row == listed[slot:slot + 1, :], counted + 1.0, counted)
        quarters.append(counted)
    own_counts_t, ghost_counts_t = jnp.concatenate(quarters[:2], axis=0), jnp.concatenate(quarters[2:], axis=0)
    count_out[:, 0:atoms] = dot_nn(own_counts_t.astype(bf16), pick_cols).T.astype(bf16)
    count_out[:, atoms:2 * atoms] = dot_nn(ghost_counts_t.astype(bf16), pick_cols).T.astype(bf16)
    for block in (3, 2, 1, 0):
        count_copy(block).start()
    spread_start(pos_all, p_send, p_recv)
    own_counts, ghost_counts = own_counts_t.T, ghost_counts_t.T

    cos_fine, sin_fine = cos_series(9), sin_series(9)
    own_cos, own_sin = turns_cos_sin(0.5 * own32, cos_fine, sin_fine)
    own_cos_col, own_sin_col = own_cos.T, own_sin.T
    embedding = emb_ref[...].astype(f32)
    gains = gain_ref[...].astype(f32)
    is_second = own32.T[:, 3:4] > 0.5
    hidden = jnp.where(is_second, embedding[1:2, :], embedding[0:1, :])
    both = lax.broadcasted_iota(jnp.int32, (16, embedding.shape[1]), 0)
    both = jnp.where(both == 1, embedding[1:2, :], embedding[0:1, :]).astype(bf16)
    projected_kinds = dot_nn(both, win_ref[0]).astype(bf16).astype(f32)
    own_feats = jnp.where(is_second, projected_kinds[1:2, :], projected_kinds[0:1, :]).astype(bf16)

    def fill_pairs(pairs, counts, table_cos, table_sin):
        chord = jnp.zeros((atoms, atoms), f32)
        for d in range(3):
            apart = table_sin[d:d + 1, :] * own_cos_col[:, d:d + 1] - table_cos[d:d + 1, :] * own_sin_col[:, d:d + 1]
            chord = chord + apart * apart
        basis = jnp.exp(-0.125 * chord)
        for b in range(bases):
            pair = counts * basis
            high = pair.astype(bf16)
            rows = slice(b * atoms, (b + 1) * atoms)
            pairs[rows, 0:atoms] = high
            pairs[rows, atoms:2 * atoms] = (pair - high.astype(f32)).astype(bf16)
            basis = basis * basis

    def messages(number, pairs, feats):
        return radial_sum(number, dot_nn(pairs[...], jnp.concatenate([feats, feats], axis=0)))

    def radial_sum(number, products):
        radial_layer = rad_ref[number].astype(f32)
        message = radial_layer[0:1, :] * products[:atoms]
        for b in range(1, bases):
            message = message + radial_layer[b:b + 1, :] * products[b * atoms:(b + 1) * atoms]
        return message

    def update(number, hidden, message):
        normed = message * lax.rsqrt(jnp.mean(message * message, axis=1, keepdims=True) + epsilon)
        normed = normed * gains[number:number + 1, :]
        activated = (normed / (1.0 + jnp.exp(-normed))).astype(bf16)
        return (hidden + dot_nn(activated, wout_ref[number])).astype(bf16)

    fill_pairs(pairs_own, own_counts, own_cos, own_sin)
    own_message = messages(0, pairs_own, own_feats)

    wv32[...] = jnp.zeros_like(wv32)
    for slot in range(members):
        dx, dy, _ = chip_offsets[slot % plane]
        chip = lax.rem(my_x + dx, side) * side + lax.rem(my_y + dy, side)
        owner = (core if slot < plane else 1 - core) * plane + chip
        wv32[0:3, share_lanes(slot, 1)] = wv_ref[:, pl.ds(pl.multiple_of(owner * share, 128), share)].astype(f32)
    own_waves = wv32[:, share_lanes(0, 1)]
    waves8 = own_waves.astype(bf16)

    def share_phases(step):
        for part in range(8):
            rows = pl.ds(pl.multiple_of(step * 1024 + part * 128, 128), 128)
            places = pos_all[:, rows].astype(f32).T.astype(bf16)
            cosines, sines = phase_pair(dot_nn(places, waves8))
            share_phase[rows, 0:share] = cosines.astype(bf16)
            share_phase[rows, share:2 * share] = sines.astype(bf16)

    def atom_phases(step):
        for part in range(8):
            rows = pl.ds(pl.multiple_of(step * 2048 + part * 256, 256), 256)
            cosines, sines = phase_pair(dot_nn(wv32[:, rows].T.astype(bf16), own_coords))
            atom_phase[rows, 0:atoms] = cosines.astype(bf16)
            atom_phase[rows, atoms:2 * atoms] = sines.astype(bf16)

    squared = jnp.sum(own_waves * own_waves, axis=0, keepdims=True)
    kweight = jnp.exp(-smearing * squared) / squared * scale

    pl.loop(0, 2)(atom_phases)
    tiles_all.wait_recv()
    near_all.wait_recv()
    lane_block = lax.broadcasted_iota(jnp.int32, (8, atoms), 1) // ghosts

    def ghosts_of(step):
        merged = jnp.zeros((8, atoms), f32)
        for block in range(4):
            source = place((step[0] + steps[block][0], step[1] + steps[block][1]))
            merged = jnp.where(lane_block == block, tiles[tile_of[source]].astype(f32), merged)
        return merged

    ghost32 = ghosts_of((0, 0))
    tables = [ghost32] + [near_coords[block].astype(f32) for block in range(4)] + [ghosts_of(step) for step in steps]
    table_cos, table_sin = turns_cos_sin(0.5 * jnp.concatenate(tables, axis=0), cos_fine, sin_fine)
    ghost_cos, ghost_sin = table_cos[0:8], table_sin[0:8]
    fill_pairs(pairs_ghost, ghost_counts, ghost_cos, ghost_sin)
    ghost_second = ghost32.T[:, 3:4] > 0.5
    ghost_feats = jnp.where(ghost_second, projected_kinds[1:2, :], projected_kinds[0:1, :]).astype(bf16)

    ghost_cos_col, ghost_sin_col = ghost_cos.T, ghost_sin.T
    count_all.wait_recv()
    halves = []
    for half in range(2):
        chords, kinds = [], []
        for block in range(4):
            entry = 1 + half * 4 + block
            rows = slice(block * ghosts, (block + 1) * ghosts)
            chord = jnp.zeros((ghosts, atoms), f32)
            for d in range(3):
                at = entry * 8 + d
                apart = table_sin[at:at + 1, :] * ghost_cos_col[rows, d:d + 1] - table_cos[at:at + 1, :] * ghost_sin_col[rows, d:d + 1]
                chord = chord + apart * apart
            chords.append(chord)
            kinds.append(jnp.broadcast_to(tables[entry][3:4, :], (ghosts, atoms)))
        basis = jnp.exp(-0.125 * jnp.concatenate(chords, axis=0))
        halves.append([basis, count_in[:, half * atoms:(half + 1) * atoms].astype(f32), jnp.concatenate(kinds, axis=0)])
    for b in range(bases):
        pair0, pair1 = (basis * counts for basis, counts, _ in halves)
        second = pair0 * halves[0][2] + pair1 * halves[1][2]
        first = pair0 + pair1 - second
        rows = slice(b * atoms, (b + 1) * atoms)
        for number, part in enumerate((first, second)):
            high = part.astype(bf16)
            pairs_kind[rows, 2 * number * atoms:(2 * number + 1) * atoms] = high
            pairs_kind[rows, (2 * number + 1) * atoms:(2 * number + 2) * atoms] = (part - high.astype(f32)).astype(bf16)
        for half in halves:
            half[0] = half[0] * half[0]
    kind_rows = jnp.concatenate(
        [jnp.broadcast_to(projected_kinds[kind:kind + 1, :], (2 * atoms, projected_kinds.shape[1])) for kind in range(2)],
        axis=0).astype(bf16)
    ghost_message = radial_sum(0, dot_nn(pairs_kind[...], kind_rows))
    message = jnp.concatenate([own_message + messages(0, pairs_ghost, ghost_feats), ghost_message], axis=0)
    ghost_hidden = jnp.where(ghost_second, embedding[1:2, :], embedding[0:1, :])
    everyone = update(0, jnp.concatenate([hidden, ghost_hidden], axis=0), message)
    hidden = everyone[:atoms]
    projected = dot_nn(everyone, win_ref[1]).astype(bf16)
    message = messages(1, pairs_own, projected[:atoms]) + messages(1, pairs_ghost, projected[atoms:])
    hidden = update(1, hidden, message)
    charges = dot_nt(wch_ref[...], hidden)
    q_all[:, 0:atoms] = charges.astype(bf16)
    spread_start(q_all, q_send, q_recv)
    tiles_all.wait_send()
    near_all.wait_send()
    count_all.wait_send()

    spread_near(pos_all, p_send, p_recv)
    spread_far(pos_all, p_send, p_recv)
    pl.loop(0, 4)(share_phases)
    spread_sent(pos_all, p_send, p_recv)

    near_lanes, far_lanes = slice(0, near_count * atoms), slice(near_count * atoms, members * atoms)
    spread_near(q_all, q_send, q_recv)
    both_parts = dot_nn(q_all[:, near_lanes], share_phase[near_lanes, :])
    spread_far(q_all, q_send, q_recv)
    both_parts = both_parts + dot_nn(q_all[:, far_lanes], share_phase[far_lanes, :])
    z_out[...] = (jnp.concatenate([both_parts[:, :share], both_parts[:, share:]], axis=0) * kweight).astype(bf16)
    for dz in heights:
        column_copy(dz).start()
    pl.loop(2, 6)(atom_phases)
    spread_sent(q_all, q_send, q_recv)

    column_all.wait_recv()
    summed = z_out[...].astype(f32)
    for dz in range(1, depth):
        summed = summed + z_in[dz - 1].astype(f32)
    z_full[:, share_lanes(0, 1)] = summed.astype(bf16)
    for number in range(plane - 1, 0, -1):
        plane_copy(number).start()
    twin_copy(0).start()
    column_all.wait_send()

    def apply_slots(first, last):
        for slot in range(first, last):
            lanes = share_lanes(slot, 1)
            block = z_full[:, lanes]
            left[0:16, lanes] = block
            block = block.astype(f32)
            waves = wv32[:, lanes]
            for d in range(3):
                left[16 * (d + 1):16 * (d + 2), lanes] = (block * waves[d:d + 1, :]).astype(bf16)
        lanes = share_lanes(first, last - first)
        return dot_nn(left[:, lanes], atom_phase[lanes, :])

    def take_ring(ring):
        for slot in range(max(rings[ring][0], 1), rings[ring][1]):
            plane_arrival(slot).wait_recv()
            twin_copy(slot).start()

    def take_twin_ring(ring):
        twin_arrival(ring).wait_recv()
        return apply_slots(plane + rings[ring][0], plane + rings[ring][1])

    take_ring(0)
    take_ring(1)
    sums = apply_slots(*rings[0])
    take_ring(2)
    sums = sums + apply_slots(*rings[1])
    sums = sums + take_twin_ring(0)
    sums = sums + apply_slots(*rings[2])
    sums = sums + take_twin_ring(1)
    sums = sums + take_twin_ring(2)
    plane_all.wait_send()
    by_cos, by_sin = sums[:, :atoms], sums[:, atoms:]
    pot_ref[...] = by_cos[:latent] + by_sin[latent:2 * latent]
    for d in range(3):
        first = 2 * latent * (d + 1)
        inner = by_sin[first:first + latent] - by_cos[first + latent:first + 2 * latent]
        force_ref[d:d + 1, :] = jnp.sum(charges * inner, axis=0, keepdims=True)
    twin_all.wait_send()


def per_device(positions, species, neighbours, ghost_rows, wavevectors, embedding, w_in, radial, norm_gain, w_out, w_charge):
    atoms = positions.shape[1]
    total_k = wavevectors.shape[1]
    latent = w_charge.shape[1]
    bases = radial.shape[1]
    share = total_k // members
    scale = 1.0 / math.sqrt(atoms * lax.axis_size(("dom", "sub")))
    operands = (
        positions, species.reshape(1, atoms), ghost_rows, neighbours, wavevectors,
        embedding, w_in, radial, norm_gain, w_out, w_charge.T,
    )
    dma = pltpu.SemaphoreType.DMA
    vmem = pl.BlockSpec(memory_space=pltpu.VMEM)
    hbm = pl.BlockSpec(memory_space=pltpu.HBM)
    return pl.pallas_call(
        functools.partial(kernel, scale),
        out_shape=(jax.ShapeDtypeStruct((latent, atoms), f32), jax.ShapeDtypeStruct((3, atoms), f32)),
        in_specs=[hbm] * len(operands),
        out_specs=(vmem, vmem),
        scratch_shapes=[pltpu.VMEM(value.shape, value.dtype) for value in operands] + [
            pltpu.VMEM((8, atoms), f32),
            pltpu.VMEM((12, 8, atoms), bf16),
            pltpu.VMEM((4, 8, atoms), bf16),
            pltpu.VMEM((8, atoms), f32),
            pltpu.VMEM((8, members * atoms), bf16),
            pltpu.VMEM((latent, members * atoms), bf16),
            pltpu.VMEM((8, total_k), f32),
            pltpu.VMEM((members * atoms, 2 * share), bf16),
            pltpu.VMEM((total_k, 2 * atoms), bf16),
            pltpu.VMEM((bases * atoms, 2 * atoms), bf16),
            pltpu.VMEM((bases * atoms, 2 * atoms), bf16),
            pltpu.VMEM((bases * atoms, 4 * atoms), bf16),
            pltpu.VMEM((atoms, 2 * atoms), bf16),
            pltpu.VMEM((atoms, 2 * atoms), bf16),
            pltpu.VMEM((16, share), bf16),
            pltpu.VMEM((depth - 1, 16, share), bf16),
            pltpu.VMEM((16, total_k), bf16),
            pltpu.VMEM((64, total_k), bf16),
            dma((len(operands),)), dma, dma, dma, dma, dma, dma, dma, dma((2,)), dma, dma((2,)),
            dma, dma, dma, dma((plane,)), dma, dma((3,)),
        ],
        compiler_params=pltpu.CompilerParams(
            collective_id=0, has_side_effects=True, vmem_limit_bytes=48 * 1024 * 1024
        ),
        name="ewald_step",
    )(*[pltpu.with_memory_space_constraint(value, pltpu.HBM) for value in operands])


def solution(mesh):
    return jax.shard_map(
        per_device,
        mesh=mesh,
        in_specs=(
            P(None, ("dom", "sub")),
            P(("dom", "sub")),
            P(None, ("dom", "sub")),
            P(None, ("dom", "sub")),
            P(),
            P(),
            P(),
            P(),
            P(),
            P(),
            P(),
        ),
        out_specs=(P(None, ("dom", "sub")), P(None, ("dom", "sub"))),
        check_vma=False,
    )
```

```python
import functools
import math

import jax
import jax.numpy as jnp
import numpy as np
from jax import lax
from jax.experimental import pallas as pl
from jax.experimental.pallas import tpu as pltpu
from jax.sharding import PartitionSpec as P

MESH = pl.DeviceIdType.MESH
smearing = 0.005
epsilon = 1e-05
f32 = jnp.float32
bf16 = jnp.bfloat16
side = 4
plane = side * side
members = 2 * plane
depth = 8
round_magic = 12582912.0


def fit_series(function, terms):
    nodes = (np.cos(np.pi * (np.arange(4 * terms) + 0.5) / (4 * terms)) + 1.0) / 8.0
    fitted = np.polynomial.chebyshev.Chebyshev.fit(nodes, function(np.sqrt(nodes)), terms - 1, domain=[0.0, 0.25])
    return [float(c) for c in fitted.convert(kind=np.polynomial.Polynomial).coef]


def cos_series(terms):
    return fit_series(lambda t: np.cos(2.0 * np.pi * t), terms)


def sin_series(terms):
    return fit_series(lambda t: np.sin(2.0 * np.pi * t) / t, terms)


half_sin = fit_series(lambda t: math.sqrt(2.0) * np.sin(np.pi * t) / t, 4)
half_cos = fit_series(lambda t: math.sqrt(2.0) * np.cos(np.pi * t), 4)


def horner(coefs, u):
    value = coefs[-1]
    for c in coefs[-2::-1]:
        value = value * u + c
    return value


def turns_cos_sin(turns, cos_coefs, sin_coefs):
    t = turns - ((turns + round_magic) - round_magic)
    u = t * t
    return horner(cos_coefs, u), t * horner(sin_coefs, u)


def phase_pair(turns):
    t = turns - ((turns + round_magic) - round_magic)
    u = t * t
    s = t * horner(half_sin, u)
    return 1.0 - s * s, s * horner(half_cos, u)


def dot_nt(a, b):
    return lax.dot_general(a, b, (((1,), (1,)), ((), ())), preferred_element_type=f32)


def dot_nn(a, b):
    return jnp.dot(a, b, preferred_element_type=f32)


def torus_offsets():
    every = [(dx, dy, dc) for dx in range(side) for dy in range(side) for dc in range(2)]
    return sorted(every, key=lambda o: (min(o[0], side - o[0]) + min(o[1], side - o[1]), o))


def opposite(offset):
    return (-offset[0] % side, -offset[1] % side, offset[2])


def kernel(
    scale,
    pos_hbm, spec_hbm, gr_hbm, nbr_hbm, wv_hbm, emb_hbm, win_hbm, rad_hbm, gain_hbm, wout_hbm, wch_hbm,
    pot_ref, force_ref,
    pos_ref, spec_ref, gr_ref, nbr_ref, wv_ref, emb_ref, win_ref, rad_ref, gain_ref, wout_ref, wch_ref,
    c32, tiles, near_coords, gpad, pos_all, q_all, wv32,
    share_phase, atom_phase, pairs_own, pairs_ghost, pairs_kind, count_out, count_in, z_out, z_in, z_full, left,
    in_sem, g1_send, g1_recv, g2_send, g2_recv, g3_send, g3_recv, p_send, p_recv, q_send, q_recv,
    zs_send, zs_recv, w_send, w_recv, x_send, x_recv,
):
    dom = lax.axis_index("dom")
    sub = lax.axis_index("sub")
    n_dom = lax.axis_size("dom")
    n_sub = lax.axis_size("sub")
    zl, xy = dom // plane, lax.rem(dom, plane)
    my_x, my_y = xy // side, lax.rem(xy, side)
    zh, core = sub // 2, lax.rem(sub, 2)
    z_me = zh * (depth // 2) + zl
    atoms = pos_ref.shape[1]
    total_k = wv_ref.shape[1]
    share = total_k // members
    latent = wch_ref.shape[0]
    bases = rad_ref.shape[1]
    ghosts = gr_ref.shape[1]

    def member(offset):
        dx, dy, dc = offset
        chip = lax.rem(my_x + dx, side) * side + lax.rem(my_y + dy, side)
        return (zl * plane + chip, zh * 2 + (1 - core if dc else core))

    def column_member(dz):
        index = lax.rem(z_me + dz, depth)
        return (lax.rem(index, depth // 2) * plane + xy, (index // (depth // 2)) * 2 + core)

    steps = ((-1, 0), (1, 0), (0, -1), (0, 1))
    around = ((0, -1), (0, 1), (-1, -1), (-1, 1), (1, -1), (1, 1), (0, 2), (-1, 0), (1, 0), (-2, 0), (2, 0))

    def place(step):
        return (step[0], step[1] % 4)

    def beside(step):
        return (lax.rem(dom + step[0] + n_dom, n_dom), lax.rem(sub + step[1] + n_sub, n_sub))

    def reverse(step):
        return (-step[0], -step[1])

    tile_of = {place(step): number for number, step in enumerate(around)}
    tile_of[(0, 0)] = len(around)
    neighbours_at = tuple(beside(reverse(step)) for step in steps)
    offsets = torus_offsets()
    slot_of = {offset: slot for slot, offset in enumerate(offsets)}
    chip_offsets = [offset for offset in offsets if offset[2] == 0]
    heights = sorted(range(1, depth), key=lambda dz: -min(dz, depth - dz))

    fetches = [
        pltpu.make_async_copy(source, target, in_sem.at[number])
        for number, (source, target) in enumerate((
            (pos_hbm, pos_ref), (spec_hbm, spec_ref), (gr_hbm, gr_ref), (nbr_hbm, nbr_ref), (wv_hbm, wv_ref),
            (emb_hbm, emb_ref), (win_hbm, win_ref), (rad_hbm, rad_ref), (gain_hbm, gain_ref), (wout_hbm, wout_ref),
            (wch_hbm, wch_ref)))
    ]
    barrier = pltpu.get_barrier_semaphore()

    def greet(target):
        pl.semaphore_signal(barrier, inc=1, device_id=target, device_id_type=MESH)

    for step in around:
        greet(beside(step))
    for fetch in fetches[:3]:
        fetch.start()
    for offset in offsets[:0:-1]:
        greet(member(offset))
    for dz in heights:
        greet(column_member(dz))
    for fetch in fetches[3:]:
        fetch.start()

    c32[...] = jnp.zeros_like(c32)
    gpad[...] = jnp.zeros_like(gpad)
    for fetch in fetches[:3]:
        fetch.wait()
    c32[0:3, :] = pos_ref[...].astype(f32)
    c32[3:4, :] = spec_ref[...].astype(f32)
    own32 = c32[...]
    own_coords = own32.astype(bf16)
    gpad[0:4, 0:ghosts] = gr_ref[...].astype(f32)
    grown = gpad[...]
    picks = grown[1:2, :]
    for block, source in ((1, 0), (2, 3), (3, 2)):
        picks = picks + pltpu.roll(grown, block * ghosts, axis=1)[source:source + 1, :]
    row_number = lax.broadcasted_iota(jnp.int32, (atoms, atoms), 0).astype(f32)
    pick_cols = jnp.where(row_number == picks, 1.0, 0.0)
    pick_cols = pick_cols.astype(bf16)
    tiles[len(around)] = dot_nn(own_coords, pick_cols).astype(bf16)
    pos_all[:, 0:atoms] = own_coords

    def tile_copy(step):
        return pltpu.make_async_remote_copy(
            src_ref=tiles.at[len(around)], dst_ref=tiles.at[tile_of[place(reverse(step))]], send_sem=g1_send,
            recv_sem=g1_recv, device_id=beside(step), device_id_type=MESH)

    def near_copy(block):
        return pltpu.make_async_remote_copy(
            src_ref=pos_all.at[:, pl.ds(0, atoms)], dst_ref=near_coords.at[block], send_sem=g2_send, recv_sem=g2_recv,
            device_id=neighbours_at[block], device_id_type=MESH)

    def count_copy(block):
        rows = pl.ds(block * ghosts, ghosts)
        return pltpu.make_async_remote_copy(
            src_ref=count_out.at[rows], dst_ref=count_in.at[rows], send_sem=g3_send, recv_sem=g3_recv,
            device_id=neighbours_at[block], device_id_type=MESH)

    def slot_lanes(first, count):
        return pl.ds(first * atoms, count * atoms)

    near_count = members // 2

    def spread_copy(buffer, send, recv, offset):
        landing = slot_of[opposite(offset)]
        return pltpu.make_async_remote_copy(
            src_ref=buffer.at[:, slot_lanes(0, 1)], dst_ref=buffer.at[:, slot_lanes(landing, 1)],
            send_sem=send, recv_sem=recv.at[0 if landing < near_count else 1],
            device_id=member(offset), device_id_type=MESH)

    def spread_all(buffer, send, recv, first, count, group):
        lanes = slot_lanes(first, count)
        return pltpu.make_async_remote_copy(
            src_ref=buffer.at[:, lanes], dst_ref=buffer.at[:, lanes], send_sem=send, recv_sem=recv.at[group],
            device_id=member(offsets[1]), device_id_type=MESH)

    def spread_start(buffer, send, recv):
        for offset in offsets[:0:-1]:
            spread_copy(buffer, send, recv, offset).start()

    def spread_near(buffer, send, recv):
        spread_all(buffer, send, recv, 1, near_count - 1, 0).wait_recv()

    def spread_far(buffer, send, recv):
        spread_all(buffer, send, recv, near_count, members - near_count, 1).wait_recv()

    def spread_sent(buffer, send, recv):
        spread_all(buffer, send, recv, 1, members - 1, 0).wait_send()

    def column_copy(dz):
        return pltpu.make_async_remote_copy(
            src_ref=z_out, dst_ref=z_in.at[dz - 1], send_sem=zs_send, recv_sem=zs_recv,
            device_id=column_member(dz), device_id_type=MESH)

    column_all = pltpu.make_async_remote_copy(
        src_ref=z_in, dst_ref=z_in, send_sem=zs_send, recv_sem=zs_recv,
        device_id=column_member(1), device_id_type=MESH)

    def share_lanes(first, count):
        return pl.ds(first * share, count * share)

    def plane_copy(number):
        landing = chip_offsets.index(opposite(chip_offsets[number]))
        return pltpu.make_async_remote_copy(
            src_ref=z_full.at[:, share_lanes(0, 1)], dst_ref=z_full.at[:, share_lanes(landing, 1)],
            send_sem=w_send, recv_sem=w_recv.at[landing], device_id=member(chip_offsets[number]), device_id_type=MESH)

    def plane_arrival(slot):
        lanes = share_lanes(slot, 1)
        return pltpu.make_async_remote_copy(
            src_ref=z_full.at[:, lanes], dst_ref=z_full.at[:, lanes], send_sem=w_send, recv_sem=w_recv.at[slot],
            device_id=member(chip_offsets[1]), device_id_type=MESH)

    plane_all = pltpu.make_async_remote_copy(
        src_ref=z_full.at[:, share_lanes(1, plane - 1)], dst_ref=z_full.at[:, share_lanes(1, plane - 1)],
        send_sem=w_send, recv_sem=w_recv.at[0], device_id=member(chip_offsets[1]), device_id_type=MESH)
    twin = (dom, zh * 2 + 1 - core)
    rings = ((0, 5), (5, 11), (11, plane))

    def twin_copy(slot):
        ring = [first <= slot < last for first, last in rings].index(True)
        return pltpu.make_async_remote_copy(
            src_ref=z_full.at[:, share_lanes(slot, 1)], dst_ref=z_full.at[:, share_lanes(plane + slot, 1)],
            send_sem=x_send, recv_sem=x_recv.at[ring], device_id=twin, device_id_type=MESH)

    def twin_arrival(ring):
        first, last = rings[ring]
        lanes = share_lanes(plane + first, last - first)
        return pltpu.make_async_remote_copy(
            src_ref=z_full.at[:, lanes], dst_ref=z_full.at[:, lanes], send_sem=x_send, recv_sem=x_recv.at[ring],
            device_id=twin, device_id_type=MESH)

    twin_all = pltpu.make_async_remote_copy(
        src_ref=z_full.at[:, share_lanes(0, plane)], dst_ref=z_full.at[:, share_lanes(0, plane)],
        send_sem=x_send, recv_sem=x_recv.at[0], device_id=twin, device_id_type=MESH)
    tiles_all = pltpu.make_async_remote_copy(
        src_ref=tiles.at[pl.ds(0, len(around))], dst_ref=tiles.at[pl.ds(0, len(around))], send_sem=g1_send,
        recv_sem=g1_recv, device_id=twin, device_id_type=MESH)
    near_all = pltpu.make_async_remote_copy(
        src_ref=near_coords, dst_ref=near_coords, send_sem=g2_send, recv_sem=g2_recv, device_id=twin, device_id_type=MESH)
    count_all = pltpu.make_async_remote_copy(
        src_ref=count_in, dst_ref=count_in, send_sem=g3_send, recv_sem=g3_recv, device_id=twin, device_id_type=MESH)

    pl.semaphore_wait(barrier, len(around) + (members - 1) + (depth - 1))
    for step in around:
        tile_copy(step).start()
    for block in (3, 2, 1, 0):
        near_copy(block).start()

    for fetch in fetches[3:]:
        fetch.wait()
    listed = nbr_ref[...]
    quarters = []
    for first in range(0, 2 * atoms, 64):
        table_row = lax.broadcasted_iota(jnp.int32, (64, atoms), 0) + first
        counted = jnp.zeros((64, atoms), f32)
        for slot in range(listed.shape[0]):
            counted = jnp.where(table_row == listed[slot:slot + 1, :], counted + 1.0, counted)
        quarters.append(counted)
    own_counts_t, ghost_counts_t = jnp.concatenate(quarters[:2], axis=0), jnp.concatenate(quarters[2:], axis=0)
    count_out[:, 0:atoms] = dot_nn(own_counts_t.astype(bf16), pick_cols).T.astype(bf16)
    count_out[:, atoms:2 * atoms] = dot_nn(ghost_counts_t.astype(bf16), pick_cols).T.astype(bf16)
    for block in (3, 2, 1, 0):
        count_copy(block).start()
    spread_start(pos_all, p_send, p_recv)
    own_counts, ghost_counts = own_counts_t.T, ghost_counts_t.T

    cos_fine, sin_fine = cos_series(9), sin_series(9)
    own_cos, own_sin = turns_cos_sin(0.5 * own32, cos_fine, sin_fine)
    own_cos_col, own_sin_col = own_cos.T, own_sin.T
    embedding = emb_ref[...].astype(f32)
    gains = gain_ref[...].astype(f32)
    is_second = own32.T[:, 3:4] > 0.5
    hidden = jnp.where(is_second, embedding[1:2, :], embedding[0:1, :])
    both = lax.broadcasted_iota(jnp.int32, (16, embedding.shape[1]), 0)
    both = jnp.where(both == 1, embedding[1:2, :], embedding[0:1, :]).astype(bf16)
    projected_kinds = dot_nn(both, win_ref[0]).astype(bf16).astype(f32)
    own_feats = jnp.where(is_second, projected_kinds[1:2, :], projected_kinds[0:1, :]).astype(bf16)

    def fill_pairs(pairs, counts, table_cos, table_sin):
        chord = jnp.zeros((atoms, atoms), f32)
        for d in range(3):
            apart = table_sin[d:d + 1, :] * own_cos_col[:, d:d + 1] - table_cos[d:d + 1, :] * own_sin_col[:, d:d + 1]
            chord = chord + apart * apart
        basis = jnp.exp(-0.125 * chord)
        for b in range(bases):
            pair = counts * basis
            high = pair.astype(bf16)
            rows = slice(b * atoms, (b + 1) * atoms)
            pairs[rows, 0:atoms] = high
            pairs[rows, atoms:2 * atoms] = (pair - high.astype(f32)).astype(bf16)
            basis = basis * basis

    def messages(number, pairs, feats):
        return radial_sum(number, dot_nn(pairs[...], jnp.concatenate([feats, feats], axis=0)))

    def radial_sum(number, products):
        radial_layer = rad_ref[number].astype(f32)
        message = radial_layer[0:1, :] * products[:atoms]
        for b in range(1, bases):
            message = message + radial_layer[b:b + 1, :] * products[b * atoms:(b + 1) * atoms]
        return message

    def update(number, hidden, message):
        normed = message * lax.rsqrt(jnp.mean(message * message, axis=1, keepdims=True) + epsilon)
        normed = normed * gains[number:number + 1, :]
        activated = (normed / (1.0 + jnp.exp(-normed))).astype(bf16)
        return (hidden + dot_nn(activated, wout_ref[number])).astype(bf16)

    fill_pairs(pairs_own, own_counts, own_cos, own_sin)
    own_message = messages(0, pairs_own, own_feats)

    wv32[...] = jnp.zeros_like(wv32)
    for slot in range(members):
        dx, dy, _ = chip_offsets[slot % plane]
        chip = lax.rem(my_x + dx, side) * side + lax.rem(my_y + dy, side)
        owner = (core if slot < plane else 1 - core) * plane + chip
        wv32[0:3, share_lanes(slot, 1)] = wv_ref[:, pl.ds(pl.multiple_of(owner * share, 128), share)].astype(f32)
    own_waves = wv32[:, share_lanes(0, 1)]
    waves8 = own_waves.astype(bf16)

    def share_phases(step):
        for part in range(16):
            rows = pl.ds(pl.multiple_of(step * 2048 + part * 128, 128), 128)
            places = pos_all[:, rows].astype(f32).T.astype(bf16)
            cosines, sines = phase_pair(dot_nn(places, waves8))
            share_phase[rows, 0:share] = cosines.astype(bf16)
            share_phase[rows, share:2 * share] = sines.astype(bf16)

    def atom_phases(step):
        for part in range(8):
            rows = pl.ds(pl.multiple_of(step * 2048 + part * 256, 256), 256)
            cosines, sines = phase_pair(dot_nn(wv32[:, rows].T.astype(bf16), own_coords))
            atom_phase[rows, 0:atoms] = cosines.astype(bf16)
            atom_phase[rows, atoms:2 * atoms] = sines.astype(bf16)

    squared = jnp.sum(own_waves * own_waves, axis=0, keepdims=True)
    kweight = jnp.exp(-smearing * squared) / squared * scale

    pl.loop(0, 2)(atom_phases)
    tiles_all.wait_recv()
    near_all.wait_recv()
    lane_block = lax.broadcasted_iota(jnp.int32, (8, atoms), 1) // ghosts

    def ghosts_of(step):
        merged = jnp.zeros((8, atoms), f32)
        for block in range(4):
            source = place((step[0] + steps[block][0], step[1] + steps[block][1]))
            merged = jnp.where(lane_block == block, tiles[tile_of[source]].astype(f32), merged)
        return merged

    ghost32 = ghosts_of((0, 0))
    tables = [ghost32] + [near_coords[block].astype(f32) for block in range(4)] + [ghosts_of(step) for step in steps]
    table_cos, table_sin = turns_cos_sin(0.5 * jnp.concatenate(tables, axis=0), cos_fine, sin_fine)
    ghost_cos, ghost_sin = table_cos[0:8], table_sin[0:8]
    fill_pairs(pairs_ghost, ghost_counts, ghost_cos, ghost_sin)
    ghost_second = ghost32.T[:, 3:4] > 0.5
    ghost_feats = jnp.where(ghost_second, projected_kinds[1:2, :], projected_kinds[0:1, :]).astype(bf16)

    ghost_cos_col, ghost_sin_col = ghost_cos.T, ghost_sin.T
    count_all.wait_recv()
    halves = []
    for half in range(2):
        chords, kinds = [], []
        for block in range(4):
            entry = 1 + half * 4 + block
            rows = slice(block * ghosts, (block + 1) * ghosts)
            chord = jnp.zeros((ghosts, atoms), f32)
            for d in range(3):
                at = entry * 8 + d
                apart = table_sin[at:at + 1, :] * ghost_cos_col[rows, d:d + 1] - table_cos[at:at + 1, :] * ghost_sin_col[rows, d:d + 1]
                chord = chord + apart * apart
            chords.append(chord)
            kinds.append(jnp.broadcast_to(tables[entry][3:4, :], (ghosts, atoms)))
        basis = jnp.exp(-0.125 * jnp.concatenate(chords, axis=0))
        halves.append([basis, count_in[:, half * atoms:(half + 1) * atoms].astype(f32), jnp.concatenate(kinds, axis=0)])
    for b in range(bases):
        pair0, pair1 = (basis * counts for basis, counts, _ in halves)
        second = pair0 * halves[0][2] + pair1 * halves[1][2]
        first = pair0 + pair1 - second
        rows = slice(b * atoms, (b + 1) * atoms)
        for number, part in enumerate((first, second)):
            high = part.astype(bf16)
            pairs_kind[rows, 2 * number * atoms:(2 * number + 1) * atoms] = high
            pairs_kind[rows, (2 * number + 1) * atoms:(2 * number + 2) * atoms] = (part - high.astype(f32)).astype(bf16)
        for half in halves:
            half[0] = half[0] * half[0]
    kind_rows = jnp.concatenate(
        [jnp.broadcast_to(projected_kinds[kind:kind + 1, :], (2 * atoms, projected_kinds.shape[1])) for kind in range(2)],
        axis=0).astype(bf16)
    ghost_message = radial_sum(0, dot_nn(pairs_kind[...], kind_rows))
    message = jnp.concatenate([own_message + messages(0, pairs_ghost, ghost_feats), ghost_message], axis=0)
    ghost_hidden = jnp.where(ghost_second, embedding[1:2, :], embedding[0:1, :])
    everyone = update(0, jnp.concatenate([hidden, ghost_hidden], axis=0), message)
    hidden = everyone[:atoms]
    projected = dot_nn(everyone, win_ref[1]).astype(bf16)
    message = messages(1, pairs_own, projected[:atoms]) + messages(1, pairs_ghost, projected[atoms:])
    hidden = update(1, hidden, message)
    charges = dot_nt(wch_ref[...], hidden)
    q_all[:, 0:atoms] = charges.astype(bf16)
    spread_start(q_all, q_send, q_recv)
    tiles_all.wait_send()
    near_all.wait_send()
    count_all.wait_send()

    spread_near(pos_all, p_send, p_recv)
    spread_far(pos_all, p_send, p_recv)
    pl.loop(0, 2)(share_phases)
    spread_sent(pos_all, p_send, p_recv)

    near_lanes, far_lanes = slice(0, near_count * atoms), slice(near_count * atoms, members * atoms)
    spread_near(q_all, q_send, q_recv)
    both_parts = dot_nn(q_all[:, near_lanes], share_phase[near_lanes, :])
    spread_far(q_all, q_send, q_recv)
    both_parts = both_parts + dot_nn(q_all[:, far_lanes], share_phase[far_lanes, :])
    z_out[...] = (jnp.concatenate([both_parts[:, :share], both_parts[:, share:]], axis=0) * kweight).astype(bf16)
    for dz in heights:
        column_copy(dz).start()
    pl.loop(2, 6)(atom_phases)
    spread_sent(q_all, q_send, q_recv)

    column_all.wait_recv()
    summed = z_out[...].astype(f32)
    for dz in range(1, depth):
        summed = summed + z_in[dz - 1].astype(f32)
    z_full[:, share_lanes(0, 1)] = summed.astype(bf16)
    for number in range(plane - 1, 0, -1):
        plane_copy(number).start()
    twin_copy(0).start()
    column_all.wait_send()

    def apply_slots(first, last):
        for slot in range(first, last):
            lanes = share_lanes(slot, 1)
            block = z_full[:, lanes]
            left[0:16, lanes] = block
            block = block.astype(f32)
            waves = wv32[:, lanes]
            for d in range(3):
                left[16 * (d + 1):16 * (d + 2), lanes] = (block * waves[d:d + 1, :]).astype(bf16)
        lanes = share_lanes(first, last - first)
        return dot_nn(left[:, lanes], atom_phase[lanes, :])

    def take_ring(ring):
        for slot in range(max(rings[ring][0], 1), rings[ring][1]):
            plane_arrival(slot).wait_recv()
            twin_copy(slot).start()

    def take_twin_ring(ring):
        twin_arrival(ring).wait_recv()
        return apply_slots(plane + rings[ring][0], plane + rings[ring][1])

    take_ring(0)
    take_ring(1)
    sums = apply_slots(*rings[0])
    take_ring(2)
    sums = sums + apply_slots(*rings[1])
    sums = sums + take_twin_ring(0)
    sums = sums + apply_slots(*rings[2])
    sums = sums + take_twin_ring(1)
    sums = sums + take_twin_ring(2)
    plane_all.wait_send()
    by_cos, by_sin = sums[:, :atoms], sums[:, atoms:]
    pot_ref[...] = by_cos[:latent] + by_sin[latent:2 * latent]
    for d in range(3):
        first = 2 * latent * (d + 1)
        inner = by_sin[first:first + latent] - by_cos[first + latent:first + 2 * latent]
        force_ref[d:d + 1, :] = jnp.sum(charges * inner, axis=0, keepdims=True)
    twin_all.wait_send()


def per_device(positions, species, neighbours, ghost_rows, wavevectors, embedding, w_in, radial, norm_gain, w_out, w_charge):
    atoms = positions.shape[1]
    total_k = wavevectors.shape[1]
    latent = w_charge.shape[1]
    bases = radial.shape[1]
    share = total_k // members
    scale = 1.0 / math.sqrt(atoms * lax.axis_size(("dom", "sub")))
    operands = (
        positions, species.reshape(1, atoms), ghost_rows, neighbours, wavevectors,
        embedding, w_in, radial, norm_gain, w_out, w_charge.T,
    )
    dma = pltpu.SemaphoreType.DMA
    vmem = pl.BlockSpec(memory_space=pltpu.VMEM)
    hbm = pl.BlockSpec(memory_space=pltpu.HBM)
    return pl.pallas_call(
        functools.partial(kernel, scale),
        out_shape=(jax.ShapeDtypeStruct((latent, atoms), f32), jax.ShapeDtypeStruct((3, atoms), f32)),
        in_specs=[hbm] * len(operands),
        out_specs=(vmem, vmem),
        scratch_shapes=[pltpu.VMEM(value.shape, value.dtype) for value in operands] + [
            pltpu.VMEM((8, atoms), f32),
            pltpu.VMEM((12, 8, atoms), bf16),
            pltpu.VMEM((4, 8, atoms), bf16),
            pltpu.VMEM((8, atoms), f32),
            pltpu.VMEM((8, members * atoms), bf16),
            pltpu.VMEM((latent, members * atoms), bf16),
            pltpu.VMEM((8, total_k), f32),
            pltpu.VMEM((members * atoms, 2 * share), bf16),
            pltpu.VMEM((total_k, 2 * atoms), bf16),
            pltpu.VMEM((bases * atoms, 2 * atoms), bf16),
            pltpu.VMEM((bases * atoms, 2 * atoms), bf16),
            pltpu.VMEM((bases * atoms, 4 * atoms), bf16),
            pltpu.VMEM((atoms, 2 * atoms), bf16),
            pltpu.VMEM((atoms, 2 * atoms), bf16),
            pltpu.VMEM((16, share), bf16),
            pltpu.VMEM((depth - 1, 16, share), bf16),
            pltpu.VMEM((16, total_k), bf16),
            pltpu.VMEM((64, total_k), bf16),
            dma((len(operands),)), dma, dma, dma, dma, dma, dma, dma, dma((2,)), dma, dma((2,)),
            dma, dma, dma, dma((plane,)), dma, dma((3,)),
        ],
        compiler_params=pltpu.CompilerParams(
            collective_id=0, has_side_effects=True, vmem_limit_bytes=48 * 1024 * 1024
        ),
        name="ewald_step",
    )(*[pltpu.with_memory_space_constraint(value, pltpu.HBM) for value in operands])


def solution(mesh):
    return jax.shard_map(
        per_device,
        mesh=mesh,
        in_specs=(
            P(None, ("dom", "sub")),
            P(("dom", "sub")),
            P(None, ("dom", "sub")),
            P(None, ("dom", "sub")),
            P(),
            P(),
            P(),
            P(),
            P(),
            P(),
            P(),
        ),
        out_specs=(P(None, ("dom", "sub")), P(None, ("dom", "sub"))),
        check_vma=False,
    )
```

```python
import functools
import math

import jax
import jax.numpy as jnp
import numpy as np
from jax import lax
from jax.experimental import pallas as pl
from jax.experimental.pallas import tpu as pltpu
from jax.sharding import PartitionSpec as P

MESH = pl.DeviceIdType.MESH
smearing = 0.005
epsilon = 1e-05
f32 = jnp.float32
bf16 = jnp.bfloat16
side = 4
plane = side * side
members = 2 * plane
depth = 8
round_magic = 12582912.0


def fit_series(function, terms):
    nodes = (np.cos(np.pi * (np.arange(4 * terms) + 0.5) / (4 * terms)) + 1.0) / 8.0
    fitted = np.polynomial.chebyshev.Chebyshev.fit(nodes, function(np.sqrt(nodes)), terms - 1, domain=[0.0, 0.25])
    return [float(c) for c in fitted.convert(kind=np.polynomial.Polynomial).coef]


def cos_series(terms):
    return fit_series(lambda t: np.cos(2.0 * np.pi * t), terms)


def sin_series(terms):
    return fit_series(lambda t: np.sin(2.0 * np.pi * t) / t, terms)


half_sin = fit_series(lambda t: math.sqrt(2.0) * np.sin(np.pi * t) / t, 4)
half_cos = fit_series(lambda t: math.sqrt(2.0) * np.cos(np.pi * t), 4)


def horner(coefs, u):
    value = coefs[-1]
    for c in coefs[-2::-1]:
        value = value * u + c
    return value


def turns_cos_sin(turns, cos_coefs, sin_coefs):
    t = turns - ((turns + round_magic) - round_magic)
    u = t * t
    return horner(cos_coefs, u), t * horner(sin_coefs, u)


def phase_pair(turns):
    t = turns - ((turns + round_magic) - round_magic)
    u = t * t
    s = t * horner(half_sin, u)
    return 1.0 - s * s, s * horner(half_cos, u)


def dot_nt(a, b):
    return lax.dot_general(a, b, (((1,), (1,)), ((), ())), preferred_element_type=f32)


def dot_nn(a, b):
    return jnp.dot(a, b, preferred_element_type=f32)


def torus_offsets():
    every = [(dx, dy, dc) for dx in range(side) for dy in range(side) for dc in range(2)]
    return sorted(every, key=lambda o: (min(o[0], side - o[0]) + min(o[1], side - o[1]), o))


def opposite(offset):
    return (-offset[0] % side, -offset[1] % side, offset[2])


def kernel(
    scale,
    pos_hbm, spec_hbm, gr_hbm, nbr_hbm, wv_hbm, emb_hbm, win_hbm, rad_hbm, gain_hbm, wout_hbm, wch_hbm,
    pot_ref, force_ref,
    pos_ref, spec_ref, gr_ref, nbr_ref, wv_ref, emb_ref, win_ref, rad_ref, gain_ref, wout_ref, wch_ref,
    c32, tiles, near_coords, gpad, pos_all, q_all, wv32,
    share_phase, atom_phase, pairs_own, pairs_ghost, pairs_kind, count_out, count_in, z_out, z_in, z_full, left,
    in_sem, g1_send, g1_recv, g2_send, g2_recv, g3_send, g3_recv, p_send, p_recv, q_send, q_recv,
    zs_send, zs_recv, w_send, w_recv, x_send, x_recv,
):
    dom = lax.axis_index("dom")
    sub = lax.axis_index("sub")
    n_dom = lax.axis_size("dom")
    n_sub = lax.axis_size("sub")
    zl, xy = dom // plane, lax.rem(dom, plane)
    my_x, my_y = xy // side, lax.rem(xy, side)
    zh, core = sub // 2, lax.rem(sub, 2)
    z_me = zh * (depth // 2) + zl
    atoms = pos_ref.shape[1]
    total_k = wv_ref.shape[1]
    share = total_k // members
    latent = wch_ref.shape[0]
    bases = rad_ref.shape[1]
    ghosts = gr_ref.shape[1]

    def member(offset):
        dx, dy, dc = offset
        chip = lax.rem(my_x + dx, side) * side + lax.rem(my_y + dy, side)
        return (zl * plane + chip, zh * 2 + (1 - core if dc else core))

    def column_member(dz):
        index = lax.rem(z_me + dz, depth)
        return (lax.rem(index, depth // 2) * plane + xy, (index // (depth // 2)) * 2 + core)

    steps = ((-1, 0), (1, 0), (0, -1), (0, 1))
    around = ((0, -1), (0, 1), (-1, -1), (-1, 1), (1, -1), (1, 1), (0, 2), (-1, 0), (1, 0), (-2, 0), (2, 0))

    def place(step):
        return (step[0], step[1] % 4)

    def beside(step):
        return (lax.rem(dom + step[0] + n_dom, n_dom), lax.rem(sub + step[1] + n_sub, n_sub))

    def reverse(step):
        return (-step[0], -step[1])

    tile_of = {place(step): number for number, step in enumerate(around)}
    tile_of[(0, 0)] = len(around)
    neighbours_at = tuple(beside(reverse(step)) for step in steps)
    offsets = torus_offsets()
    slot_of = {offset: slot for slot, offset in enumerate(offsets)}
    chip_offsets = [offset for offset in offsets if offset[2] == 0]
    heights = sorted(range(1, depth), key=lambda dz: -min(dz, depth - dz))

    fetches = [
        pltpu.make_async_copy(source, target, in_sem.at[number])
        for number, (source, target) in enumerate((
            (pos_hbm, pos_ref), (spec_hbm, spec_ref), (gr_hbm, gr_ref), (nbr_hbm, nbr_ref), (wv_hbm, wv_ref),
            (emb_hbm, emb_ref), (win_hbm, win_ref), (rad_hbm, rad_ref), (gain_hbm, gain_ref), (wout_hbm, wout_ref),
            (wch_hbm, wch_ref)))
    ]
    barrier = pltpu.get_barrier_semaphore()

    def greet(target):
        pl.semaphore_signal(barrier, inc=1, device_id=target, device_id_type=MESH)

    for step in around:
        greet(beside(step))
    for fetch in fetches[:3]:
        fetch.start()
    for offset in offsets[:0:-1]:
        greet(member(offset))
    for dz in heights:
        greet(column_member(dz))
    for fetch in fetches[3:]:
        fetch.start()

    c32[...] = jnp.zeros_like(c32)
    gpad[...] = jnp.zeros_like(gpad)
    for fetch in fetches[:3]:
        fetch.wait()
    c32[0:3, :] = pos_ref[...].astype(f32)
    c32[3:4, :] = spec_ref[...].astype(f32)
    own32 = c32[...]
    own_coords = own32.astype(bf16)
    gpad[0:4, 0:ghosts] = gr_ref[...].astype(f32)
    grown = gpad[...]
    picks = grown[1:2, :]
    for block, source in ((1, 0), (2, 3), (3, 2)):
        picks = picks + pltpu.roll(grown, block * ghosts, axis=1)[source:source + 1, :]
    row_number = lax.broadcasted_iota(jnp.int32, (atoms, atoms), 0).astype(f32)
    pick_cols = jnp.where(row_number == picks, 1.0, 0.0)
    pick_cols = pick_cols.astype(bf16)
    tiles[len(around)] = dot_nn(own_coords, pick_cols).astype(bf16)
    pos_all[:, 0:atoms] = own_coords

    def tile_copy(step):
        return pltpu.make_async_remote_copy(
            src_ref=tiles.at[len(around)], dst_ref=tiles.at[tile_of[place(reverse(step))]], send_sem=g1_send,
            recv_sem=g1_recv, device_id=beside(step), device_id_type=MESH)

    def near_copy(block):
        return pltpu.make_async_remote_copy(
            src_ref=pos_all.at[:, pl.ds(0, atoms)], dst_ref=near_coords.at[block], send_sem=g2_send, recv_sem=g2_recv,
            device_id=neighbours_at[block], device_id_type=MESH)

    def count_copy(block):
        rows = pl.ds(block * ghosts, ghosts)
        return pltpu.make_async_remote_copy(
            src_ref=count_out.at[rows], dst_ref=count_in.at[rows], send_sem=g3_send, recv_sem=g3_recv,
            device_id=neighbours_at[block], device_id_type=MESH)

    def slot_lanes(first, count):
        return pl.ds(first * atoms, count * atoms)

    near_count = members // 2

    def spread_copy(buffer, send, recv, offset):
        landing = slot_of[opposite(offset)]
        return pltpu.make_async_remote_copy(
            src_ref=buffer.at[:, slot_lanes(0, 1)], dst_ref=buffer.at[:, slot_lanes(landing, 1)],
            send_sem=send, recv_sem=recv.at[0 if landing < near_count else 1],
            device_id=member(offset), device_id_type=MESH)

    def spread_all(buffer, send, recv, first, count, group):
        lanes = slot_lanes(first, count)
        return pltpu.make_async_remote_copy(
            src_ref=buffer.at[:, lanes], dst_ref=buffer.at[:, lanes], send_sem=send, recv_sem=recv.at[group],
            device_id=member(offsets[1]), device_id_type=MESH)

    def spread_start(buffer, send, recv):
        for offset in offsets[:0:-1]:
            spread_copy(buffer, send, recv, offset).start()

    def spread_near(buffer, send, recv):
        spread_all(buffer, send, recv, 1, near_count - 1, 0).wait_recv()

    def spread_far(buffer, send, recv):
        spread_all(buffer, send, recv, near_count, members - near_count, 1).wait_recv()

    def spread_sent(buffer, send, recv):
        spread_all(buffer, send, recv, 1, members - 1, 0).wait_send()

    def column_copy(dz):
        return pltpu.make_async_remote_copy(
            src_ref=z_out, dst_ref=z_in.at[dz - 1], send_sem=zs_send, recv_sem=zs_recv,
            device_id=column_member(dz), device_id_type=MESH)

    column_all = pltpu.make_async_remote_copy(
        src_ref=z_in, dst_ref=z_in, send_sem=zs_send, recv_sem=zs_recv,
        device_id=column_member(1), device_id_type=MESH)

    def share_lanes(first, count):
        return pl.ds(first * share, count * share)

    def plane_copy(number):
        landing = chip_offsets.index(opposite(chip_offsets[number]))
        return pltpu.make_async_remote_copy(
            src_ref=z_full.at[:, share_lanes(0, 1)], dst_ref=z_full.at[:, share_lanes(landing, 1)],
            send_sem=w_send, recv_sem=w_recv.at[landing], device_id=member(chip_offsets[number]), device_id_type=MESH)

    def plane_arrival(slot):
        lanes = share_lanes(slot, 1)
        return pltpu.make_async_remote_copy(
            src_ref=z_full.at[:, lanes], dst_ref=z_full.at[:, lanes], send_sem=w_send, recv_sem=w_recv.at[slot],
            device_id=member(chip_offsets[1]), device_id_type=MESH)

    plane_all = pltpu.make_async_remote_copy(
        src_ref=z_full.at[:, share_lanes(1, plane - 1)], dst_ref=z_full.at[:, share_lanes(1, plane - 1)],
        send_sem=w_send, recv_sem=w_recv.at[0], device_id=member(chip_offsets[1]), device_id_type=MESH)
    twin = (dom, zh * 2 + 1 - core)
    rings = ((0, 5), (5, 11), (11, plane))

    def twin_copy(slot):
        ring = [first <= slot < last for first, last in rings].index(True)
        return pltpu.make_async_remote_copy(
            src_ref=z_full.at[:, share_lanes(slot, 1)], dst_ref=z_full.at[:, share_lanes(plane + slot, 1)],
            send_sem=x_send, recv_sem=x_recv.at[ring], device_id=twin, device_id_type=MESH)

    def twin_arrival(ring):
        first, last = rings[ring]
        lanes = share_lanes(plane + first, last - first)
        return pltpu.make_async_remote_copy(
            src_ref=z_full.at[:, lanes], dst_ref=z_full.at[:, lanes], send_sem=x_send, recv_sem=x_recv.at[ring],
            device_id=twin, device_id_type=MESH)

    twin_all = pltpu.make_async_remote_copy(
        src_ref=z_full.at[:, share_lanes(0, plane)], dst_ref=z_full.at[:, share_lanes(0, plane)],
        send_sem=x_send, recv_sem=x_recv.at[0], device_id=twin, device_id_type=MESH)
    tiles_all = pltpu.make_async_remote_copy(
        src_ref=tiles.at[pl.ds(0, len(around))], dst_ref=tiles.at[pl.ds(0, len(around))], send_sem=g1_send,
        recv_sem=g1_recv, device_id=twin, device_id_type=MESH)
    near_all = pltpu.make_async_remote_copy(
        src_ref=near_coords, dst_ref=near_coords, send_sem=g2_send, recv_sem=g2_recv, device_id=twin, device_id_type=MESH)
    count_all = pltpu.make_async_remote_copy(
        src_ref=count_in, dst_ref=count_in, send_sem=g3_send, recv_sem=g3_recv, device_id=twin, device_id_type=MESH)

    pl.semaphore_wait(barrier, len(around) + (members - 1) + (depth - 1))
    for step in around:
        tile_copy(step).start()
    for block in (3, 2, 1, 0):
        near_copy(block).start()

    for fetch in fetches[3:]:
        fetch.wait()
    listed = nbr_ref[...]
    quarters = []
    for first in range(0, 2 * atoms, 64):
        table_row = lax.broadcasted_iota(jnp.int32, (64, atoms), 0) + first
        counted = jnp.zeros((64, atoms), f32)
        for slot in range(listed.shape[0]):
            counted = jnp.where(table_row == listed[slot:slot + 1, :], counted + 1.0, counted)
        quarters.append(counted)
    own_counts_t, ghost_counts_t = jnp.concatenate(quarters[:2], axis=0), jnp.concatenate(quarters[2:], axis=0)
    count_out[:, 0:atoms] = dot_nn(own_counts_t.astype(bf16), pick_cols).T.astype(bf16)
    count_out[:, atoms:2 * atoms] = dot_nn(ghost_counts_t.astype(bf16), pick_cols).T.astype(bf16)
    for block in (3, 2, 1, 0):
        count_copy(block).start()
    spread_start(pos_all, p_send, p_recv)
    own_counts, ghost_counts = own_counts_t.T, ghost_counts_t.T

    cos_fine, sin_fine = cos_series(9), sin_series(9)
    own_cos, own_sin = turns_cos_sin(0.5 * own32, cos_fine, sin_fine)
    own_cos_col, own_sin_col = own_cos.T, own_sin.T
    embedding = emb_ref[...].astype(f32)
    gains = gain_ref[...].astype(f32)
    is_second = own32.T[:, 3:4] > 0.5
    hidden = jnp.where(is_second, embedding[1:2, :], embedding[0:1, :])
    both = lax.broadcasted_iota(jnp.int32, (16, embedding.shape[1]), 0)
    both = jnp.where(both == 1, embedding[1:2, :], embedding[0:1, :]).astype(bf16)
    projected_kinds = dot_nn(both, win_ref[0]).astype(bf16).astype(f32)
    own_feats = jnp.where(is_second, projected_kinds[1:2, :], projected_kinds[0:1, :]).astype(bf16)

    def fill_pairs(pairs, counts, table_cos, table_sin):
        chord = jnp.zeros((atoms, atoms), f32)
        for d in range(3):
            apart = table_sin[d:d + 1, :] * own_cos_col[:, d:d + 1] - table_cos[d:d + 1, :] * own_sin_col[:, d:d + 1]
            chord = chord + apart * apart
        basis = jnp.exp(-0.125 * chord)
        for b in range(bases):
            pair = counts * basis
            high = pair.astype(bf16)
            rows = slice(b * atoms, (b + 1) * atoms)
            pairs[rows, 0:atoms] = high
            pairs[rows, atoms:2 * atoms] = (pair - high.astype(f32)).astype(bf16)
            basis = basis * basis

    def messages(number, pairs, feats):
        return radial_sum(number, dot_nn(pairs[...], jnp.concatenate([feats, feats], axis=0)))

    def radial_sum(number, products):
        radial_layer = rad_ref[number].astype(f32)
        message = radial_layer[0:1, :] * products[:atoms]
        for b in range(1, bases):
            message = message + radial_layer[b:b + 1, :] * products[b * atoms:(b + 1) * atoms]
        return message

    def update(number, hidden, message):
        normed = message * lax.rsqrt(jnp.mean(message * message, axis=1, keepdims=True) + epsilon)
        normed = normed * gains[number:number + 1, :]
        activated = (normed / (1.0 + jnp.exp(-normed))).astype(bf16)
        return (hidden + dot_nn(activated, wout_ref[number])).astype(bf16)

    fill_pairs(pairs_own, own_counts, own_cos, own_sin)
    own_message = messages(0, pairs_own, own_feats)

    wv32[...] = jnp.zeros_like(wv32)
    for slot in range(members):
        dx, dy, _ = chip_offsets[slot % plane]
        chip = lax.rem(my_x + dx, side) * side + lax.rem(my_y + dy, side)
        owner = (core if slot < plane else 1 - core) * plane + chip
        wv32[0:3, share_lanes(slot, 1)] = wv_ref[:, pl.ds(pl.multiple_of(owner * share, 128), share)].astype(f32)
    own_waves = wv32[:, share_lanes(0, 1)]
    waves8 = own_waves.astype(bf16)

    def share_phases(step):
        for part in range(16):
            rows = pl.ds(pl.multiple_of(step * 2048 + part * 128, 128), 128)
            places = pos_all[:, rows].astype(f32).T.astype(bf16)
            cosines, sines = phase_pair(dot_nn(places, waves8))
            share_phase[rows, 0:share] = cosines.astype(bf16)
            share_phase[rows, share:2 * share] = sines.astype(bf16)

    def atom_phases(step):
        for part in range(8):
            rows = pl.ds(pl.multiple_of(step * 2048 + part * 256, 256), 256)
            cosines, sines = phase_pair(dot_nn(wv32[:, rows].T.astype(bf16), own_coords))
            atom_phase[rows, 0:atoms] = cosines.astype(bf16)
            atom_phase[rows, atoms:2 * atoms] = sines.astype(bf16)

    squared = jnp.sum(own_waves * own_waves, axis=0, keepdims=True)
    kweight = jnp.exp(-smearing * squared) / squared * scale

    pl.loop(0, 2)(atom_phases)
    tiles_all.wait_recv()
    near_all.wait_recv()
    lane_block = lax.broadcasted_iota(jnp.int32, (8, atoms), 1) // ghosts

    def ghosts_of(step):
        merged = jnp.zeros((8, atoms), f32)
        for block in range(4):
            source = place((step[0] + steps[block][0], step[1] + steps[block][1]))
            merged = jnp.where(lane_block == block, tiles[tile_of[source]].astype(f32), merged)
        return merged

    ghost32 = ghosts_of((0, 0))
    tables = [ghost32] + [near_coords[block].astype(f32) for block in range(4)] + [ghosts_of(step) for step in steps]
    table_cos, table_sin = turns_cos_sin(0.5 * jnp.concatenate(tables, axis=0), cos_fine, sin_fine)
    ghost_cos, ghost_sin = table_cos[0:8], table_sin[0:8]
    fill_pairs(pairs_ghost, ghost_counts, ghost_cos, ghost_sin)
    ghost_second = ghost32.T[:, 3:4] > 0.5
    ghost_feats = jnp.where(ghost_second, projected_kinds[1:2, :], projected_kinds[0:1, :]).astype(bf16)

    ghost_cos_col, ghost_sin_col = ghost_cos.T, ghost_sin.T
    count_all.wait_recv()
    halves = []
    for half in range(2):
        chords, kinds = [], []
        for block in range(4):
            entry = 1 + half * 4 + block
            rows = slice(block * ghosts, (block + 1) * ghosts)
            chord = jnp.zeros((ghosts, atoms), f32)
            for d in range(3):
                at = entry * 8 + d
                apart = table_sin[at:at + 1, :] * ghost_cos_col[rows, d:d + 1] - table_cos[at:at + 1, :] * ghost_sin_col[rows, d:d + 1]
                chord = chord + apart * apart
            chords.append(chord)
            kinds.append(jnp.broadcast_to(tables[entry][3:4, :], (ghosts, atoms)))
        basis = jnp.exp(-0.125 * jnp.concatenate(chords, axis=0))
        halves.append([basis, count_in[:, half * atoms:(half + 1) * atoms].astype(f32), jnp.concatenate(kinds, axis=0)])
    for b in range(bases):
        pair0, pair1 = (basis * counts for basis, counts, _ in halves)
        second = pair0 * halves[0][2] + pair1 * halves[1][2]
        first = pair0 + pair1 - second
        rows = slice(b * atoms, (b + 1) * atoms)
        for number, part in enumerate((first, second)):
            high = part.astype(bf16)
            pairs_kind[rows, 2 * number * atoms:(2 * number + 1) * atoms] = high
            pairs_kind[rows, (2 * number + 1) * atoms:(2 * number + 2) * atoms] = (part - high.astype(f32)).astype(bf16)
        for half in halves:
            half[0] = half[0] * half[0]
    kind_rows = jnp.concatenate(
        [jnp.broadcast_to(projected_kinds[kind:kind + 1, :], (2 * atoms, projected_kinds.shape[1])) for kind in range(2)],
        axis=0).astype(bf16)
    ghost_message = radial_sum(0, dot_nn(pairs_kind[...], kind_rows))
    message = jnp.concatenate([own_message + messages(0, pairs_ghost, ghost_feats), ghost_message], axis=0)
    ghost_hidden = jnp.where(ghost_second, embedding[1:2, :], embedding[0:1, :])
    everyone = update(0, jnp.concatenate([hidden, ghost_hidden], axis=0), message)
    hidden = everyone[:atoms]
    projected = dot_nn(everyone, win_ref[1]).astype(bf16)
    message = messages(1, pairs_own, projected[:atoms]) + messages(1, pairs_ghost, projected[atoms:])
    hidden = update(1, hidden, message)
    charges = dot_nt(wch_ref[...], hidden)
    q_all[:, 0:atoms] = charges.astype(bf16)
    spread_start(q_all, q_send, q_recv)
    tiles_all.wait_send()
    near_all.wait_send()
    count_all.wait_send()

    spread_near(pos_all, p_send, p_recv)
    spread_far(pos_all, p_send, p_recv)
    pl.loop(0, 2)(share_phases)
    spread_sent(pos_all, p_send, p_recv)

    near_lanes, far_lanes = slice(0, near_count * atoms), slice(near_count * atoms, members * atoms)
    spread_near(q_all, q_send, q_recv)
    both_parts = dot_nn(q_all[:, near_lanes], share_phase[near_lanes, :])
    spread_far(q_all, q_send, q_recv)
    both_parts = both_parts + dot_nn(q_all[:, far_lanes], share_phase[far_lanes, :])
    z_out[...] = (jnp.concatenate([both_parts[:, :share], both_parts[:, share:]], axis=0) * kweight).astype(bf16)
    for dz in heights:
        column_copy(dz).start()
    pl.loop(2, 6)(atom_phases)
    spread_sent(q_all, q_send, q_recv)

    column_all.wait_recv()
    summed = z_out[...].astype(f32)
    for dz in range(1, depth):
        summed = summed + z_in[dz - 1].astype(f32)
    z_full[:, share_lanes(0, 1)] = summed.astype(bf16)
    for number in range(plane - 1, 0, -1):
        plane_copy(number).start()
    twin_copy(0).start()
    column_all.wait_send()

    def apply_slots(first, last):
        for slot in range(first, last):
            lanes = share_lanes(slot, 1)
            block = z_full[:, lanes]
            left[0:16, lanes] = block
            block = block.astype(f32)
            waves = wv32[:, lanes]
            for d in range(3):
                left[16 * (d + 1):16 * (d + 2), lanes] = (block * waves[d:d + 1, :]).astype(bf16)
        lanes = share_lanes(first, last - first)
        return dot_nn(left[:, lanes], atom_phase[lanes, :])

    def take_ring(ring):
        for slot in range(max(rings[ring][0], 1), rings[ring][1]):
            plane_arrival(slot).wait_recv()
            twin_copy(slot).start()

    def take_twin_ring(ring):
        twin_arrival(ring).wait_recv()
        return apply_slots(plane + rings[ring][0], plane + rings[ring][1])

    take_ring(0)
    take_ring(1)
    take_ring(2)
    sums = apply_slots(0, rings[1][1])
    sums = sums + take_twin_ring(0)
    sums = sums + apply_slots(*rings[2])
    sums = sums + take_twin_ring(1)
    sums = sums + take_twin_ring(2)
    plane_all.wait_send()
    by_cos, by_sin = sums[:, :atoms], sums[:, atoms:]
    pot_ref[...] = by_cos[:latent] + by_sin[latent:2 * latent]
    for d in range(3):
        first = 2 * latent * (d + 1)
        inner = by_sin[first:first + latent] - by_cos[first + latent:first + 2 * latent]
        force_ref[d:d + 1, :] = jnp.sum(charges * inner, axis=0, keepdims=True)
    twin_all.wait_send()


def per_device(positions, species, neighbours, ghost_rows, wavevectors, embedding, w_in, radial, norm_gain, w_out, w_charge):
    atoms = positions.shape[1]
    total_k = wavevectors.shape[1]
    latent = w_charge.shape[1]
    bases = radial.shape[1]
    share = total_k // members
    scale = 1.0 / math.sqrt(atoms * lax.axis_size(("dom", "sub")))
    operands = (
        positions, species.reshape(1, atoms), ghost_rows, neighbours, wavevectors,
        embedding, w_in, radial, norm_gain, w_out, w_charge.T,
    )
    dma = pltpu.SemaphoreType.DMA
    vmem = pl.BlockSpec(memory_space=pltpu.VMEM)
    hbm = pl.BlockSpec(memory_space=pltpu.HBM)
    return pl.pallas_call(
        functools.partial(kernel, scale),
        out_shape=(jax.ShapeDtypeStruct((latent, atoms), f32), jax.ShapeDtypeStruct((3, atoms), f32)),
        in_specs=[hbm] * len(operands),
        out_specs=(vmem, vmem),
        scratch_shapes=[pltpu.VMEM(value.shape, value.dtype) for value in operands] + [
            pltpu.VMEM((8, atoms), f32),
            pltpu.VMEM((12, 8, atoms), bf16),
            pltpu.VMEM((4, 8, atoms), bf16),
            pltpu.VMEM((8, atoms), f32),
            pltpu.VMEM((8, members * atoms), bf16),
            pltpu.VMEM((latent, members * atoms), bf16),
            pltpu.VMEM((8, total_k), f32),
            pltpu.VMEM((members * atoms, 2 * share), bf16),
            pltpu.VMEM((total_k, 2 * atoms), bf16),
            pltpu.VMEM((bases * atoms, 2 * atoms), bf16),
            pltpu.VMEM((bases * atoms, 2 * atoms), bf16),
            pltpu.VMEM((bases * atoms, 4 * atoms), bf16),
            pltpu.VMEM((atoms, 2 * atoms), bf16),
            pltpu.VMEM((atoms, 2 * atoms), bf16),
            pltpu.VMEM((16, share), bf16),
            pltpu.VMEM((depth - 1, 16, share), bf16),
            pltpu.VMEM((16, total_k), bf16),
            pltpu.VMEM((64, total_k), bf16),
            dma((len(operands),)), dma, dma, dma, dma, dma, dma, dma, dma((2,)), dma, dma((2,)),
            dma, dma, dma, dma((plane,)), dma, dma((3,)),
        ],
        compiler_params=pltpu.CompilerParams(
            collective_id=0, has_side_effects=True, vmem_limit_bytes=48 * 1024 * 1024
        ),
        name="ewald_step",
    )(*[pltpu.with_memory_space_constraint(value, pltpu.HBM) for value in operands])


def solution(mesh):
    return jax.shard_map(
        per_device,
        mesh=mesh,
        in_specs=(
            P(None, ("dom", "sub")),
            P(("dom", "sub")),
            P(None, ("dom", "sub")),
            P(None, ("dom", "sub")),
            P(),
            P(),
            P(),
            P(),
            P(),
            P(),
            P(),
        ),
        out_specs=(P(None, ("dom", "sub")), P(None, ("dom", "sub"))),
        check_vma=False,
    )
```
